256 devices in a mesh: dp: 16 (over y, x), key: 4 (over z_hi), tensor: 4 (over z_lo, core).
Axes of the slice: x: 4, y: 4, z: 8 (z_hi: 4, z_lo: 2; z = z_hi * 2 + z_lo), core: 2. Of those that a mesh axis runs over, the one named last changes fastest.
Arguments:
- queries: bfloat16 [16384, 8, 2, 256], P(('dp', 'key'), 'tensor'), may hold values from -6 to 6
- sub_keys: bfloat16 [1024, 8, 2, 256], P('key', 'tensor'), may hold values from -6 to 6
- query_weight: bfloat16 [4096, 4096], P(None, 'tensor'), may hold values from -0.09375 to 0.09375
- sub_choice: int32 [16384, 8, 2, 32], P(('dp', 'key'), 'tensor'), may hold values from 0 to 1023, all different within a row
- pair_choice: int32 [16384, 8, 32], P(('dp', 'key'), 'tensor'), may hold values from 0 to 1023, all different within a row
- weights: float32 [16384, 8, 32], P(('dp', 'key'), 'tensor'), may hold values from 0 to 1, as said below
- weight_grad: float32 [16384, 8, 32], P(('dp', 'key'), 'tensor'), may hold values from -6 to 6
Outputs:
- sub_key_grad: float32 [1024, 8, 2, 256], P(('dp', 'key'), 'tensor')
- input_grad: bfloat16 [16384, 4096], P(('dp', 'key', 'tensor'))
The draws below stay inside these ranges and needn't reach their ends.
Inputs may be any that keep to these rules, and one draw needn't show every extreme that they name: Each row of weights is positive and sums to one.
All inputs are finite; a program needn't handle non-finite values.
Results may differ from the reference program's by a relative error of at most 0.0058.
Values may be sent and summed in bfloat16 or wider, within the bound.
A program may use at most 64 MiB of HBM per device.

```python
import math
import jax
import jax.numpy as jnp
from jax import lax

D = 4096
HEADS = 8
NSUB = 1024
SUBW = 256
TOPK = 32
TOKENS = 16384


def draw_weights(key, part):
    scores = jax.random.normal(key, (TOKENS, HEADS, TOPK), jnp.float32) * 2.0
    return jax.nn.softmax(scores, axis=-1)


def steps_of(key, shape, pieces, low, largest):
    def one(position, blocks):
        heights = jax.random.uniform(jax.random.fold_in(jax.random.fold_in(key, 6), position), (blocks,), jnp.float32, low / len(pieces), largest / len(pieces))
        return jnp.repeat(jnp.exp(heights), shape[position] // blocks).reshape((-1,) + (1,) * (len(shape) - position - 1))

    loudness = one(*pieces[0])
    for cut in pieces[1:]:
        loudness = loudness * one(*cut)
    return loudness


def different_ones(key, rows, amount, top, lift):
    order = jax.random.permutation(jax.random.fold_in(key, 1), amount)
    boost = order
    for power in range(3):
        boost = boost * boost // amount
    boost = boost * lift // amount
    lots = jax.random.randint(jax.random.fold_in(key, 2), (rows, amount), 0, 4096) + boost
    sure = jax.random.permutation(jax.random.fold_in(key, 3), rows)[jnp.arange(amount) % rows]
    lots = jnp.where(jnp.arange(rows)[:, None] == sure[None, :], 1 << 14, lots)
    priority = lots * amount + jnp.arange(amount)
    return lax.top_k(priority.astype(jnp.int32), top)[1].astype(jnp.int32)


def centred(own_key, dims, scale, bound, cuts=(), kind=jnp.bfloat16):
    result = scale * jax.random.normal(own_key, dims, jnp.float32)
    if cuts:
        result = result * steps_of(own_key, dims, cuts, -0.22, 0.18)
    return jnp.clip(result, -bound, bound).astype(kind)


def setup_inputs(seed: int = 0) -> dict:
    key_of = jax.random.split(jax.random.key(seed), 8)
    queries = centred(key_of[0], (TOKENS, HEADS, 2, SUBW), 1.0, 6.0, ((0, 64), (1, 4)))
    sub_keys = centred(key_of[1], (NSUB, HEADS, 2, SUBW), 1.0, 6.0, ((0, 4), (1, 4)))
    query_weight = centred(key_of[2], (D, HEADS * 2 * SUBW), D ** -0.5, 0.09375, ((1, 4),))
    sub_choice = different_ones(key_of[3], TOKENS * HEADS * 2, NSUB, TOPK, 256).reshape((TOKENS, HEADS, 2, TOPK))
    pair_choice = different_ones(key_of[4], TOKENS * HEADS, TOPK * TOPK, TOPK, 0).reshape((TOKENS, HEADS, TOPK))
    weights = draw_weights(jax.random.fold_in(key_of[7], 71), 0)
    weight_grad = centred(key_of[6], (TOKENS, HEADS, TOPK), 1.0, 6.0, ((0, 64), (1, 4)), jnp.float32)
    return dict(queries=queries, sub_keys=sub_keys, query_weight=query_weight, sub_choice=sub_choice, pair_choice=pair_choice, weights=weights, weight_grad=weight_grad)


def row_table(queries_blk, sub_idx, pairs, weights, weight_grad):
    tok = pairs.shape[0]
    score_grad = weights * (weight_grad - jnp.sum(weights * weight_grad, axis=-1, keepdims=True))
    slots = jnp.arange(TOPK, dtype=jnp.int32)
    first = pairs // TOPK
    second = pairs % TOPK
    grad_one = jnp.sum(score_grad[..., None] * (first[..., None] == slots).astype(jnp.float32), axis=2)
    grad_two = jnp.sum(score_grad[..., None] * (second[..., None] == slots).astype(jnp.float32), axis=2)
    slot_grad = jnp.stack([grad_one, grad_two], axis=2)
    count = tok * HEADS * 2
    flat_grad = slot_grad.reshape(count, TOPK)
    flat_idx = sub_idx.reshape(count, TOPK).astype(jnp.int32)
    lines = jnp.arange(count, dtype=jnp.int32)[:, None]
    table = jnp.zeros((count, NSUB), jnp.float32).at[lines, flat_idx].add(flat_grad)
    return table.astype(jnp.bfloat16).reshape(tok, HEADS, 2, NSUB)


def reference(queries, sub_keys, query_weight, sub_choice, pair_choice, weights, weight_grad):
    block = math.gcd(TOKENS, 512)
    nblk = TOKENS // block

    def step(carry, index):
        start = index * block
        q_blk = lax.dynamic_slice_in_dim(queries, start, block, 0)
        s_blk = lax.dynamic_slice_in_dim(sub_choice, start, block, 0)
        p_blk = lax.dynamic_slice_in_dim(pair_choice, start, block, 0)
        w_blk = lax.dynamic_slice_in_dim(weights, start, block, 0)
        g_blk = lax.dynamic_slice_in_dim(weight_grad, start, block, 0)
        table = row_table(q_blk, s_blk, p_blk, w_blk, g_blk)
        query_grad = jnp.einsum("thxr,rhxf->thxf", table.astype(jnp.float32), sub_keys.astype(jnp.float32)).astype(jnp.bfloat16)
        carry = carry + jnp.einsum("thxr,thxf->rhxf", table.astype(jnp.float32), q_blk.astype(jnp.float32))
        flat = query_grad.reshape(block, HEADS * 2 * SUBW)
        out_blk = lax.dot_general(flat, query_weight, (((1,), (1,)), ((), ())), preferred_element_type=jnp.float32)
        return carry, out_blk.astype(jnp.bfloat16)

    start_grad = jnp.zeros((NSUB, HEADS, 2, SUBW), jnp.float32)
    sub_key_grad, blocks = lax.scan(step, start_grad, jnp.arange(nblk, dtype=jnp.int32))
    return sub_key_grad, blocks.reshape(TOKENS, D)
```

```python
import functools

import jax
import jax.numpy as jnp
from jax import lax
from jax.experimental import pallas as pl
from jax.experimental.pallas import tpu as pltpu
from jax.sharding import Mesh
from jax.sharding import PartitionSpec as P

DP_KEY = ("dp_0", "dp_1", "key")
DP_KEY_TENSOR = ("dp_0", "dp_1", "key", "tensor")
AXES = ("dp_0", "dp_1", "key", "tensor")
MESH = pl.DeviceIdType.MESH
F32 = jnp.float32
BF16 = jnp.bfloat16
CHUNKS = 8
MESSAGES = 96


def kernel(
    idx_ref, pair_ref, w_ref, wg_ref, q_ref, ks_ref, wq_ref,
    key_out, in_out,
    idxf, val, score, first, second, table, part, kbuf, wv, qg,
    r1, s3, res1, r2, s23, res2, r3, po, c1, c2s, c2r,
    w_sem, send_sem, recv_sem,
):
    y, x, k, t = (lax.axis_index(a) for a in AXES)
    zl, c = t // 2, lax.rem(t, 2)
    coord = {"dp_0": y, "dp_1": x, "key": k}

    def at(axis, step):
        return lax.rem(coord[axis] + step + 4, 4)

    def near(axis, step):
        return {axis: at(axis, step)}

    other_core = {"tensor": zl * 2 + (1 - c)}
    other_chip = {"tensor": (1 - zl) * 2 + c}

    barrier = pltpu.get_barrier_semaphore()
    partners = [near(a, s) for a in ("dp_0", "dp_1") for s in (1, -1)]
    partners += [near("key", s) for s in (1, -1, 2)] + [other_core, other_chip]
    for device in partners:
        pl.semaphore_signal(barrier, inc=1, device_id=device, device_id_type=MESH)
    pl.semaphore_wait(barrier, len(partners))

    names, sent = {}, []

    def number(name):
        return names.setdefault(name, len(names))

    def copy(name, src, dst, device):
        n = number(name)
        return pltpu.make_async_remote_copy(
            src_ref=src, dst_ref=dst, send_sem=send_sem.at[n], recv_sem=recv_sem.at[n],
            device_id=device, device_id_type=MESH,
        )

    def send(name, src, dst, device):
        one = copy(name, src, dst, device)
        one.start()
        sent.append(one)

    def arrived(name, dst):
        copy(name, dst, dst, other_core).wait_recv()

    wide = wv.shape[0] // CHUNKS
    loads = [
        pltpu.make_async_copy(wq_ref.at[pl.ds(j * wide, wide)], wv.at[pl.ds(j * wide, wide)], w_sem.at[j])
        for j in range(CHUNKS)
    ]
    for load in loads:
        load.start()

    rows = kbuf.shape[2] // 4
    spread = (("dp_1", 0), ("dp_0", 2))

    def quarter(axis, step=0):
        return pl.ds(pl.multiple_of(at(axis, step) * rows, rows), rows)

    for axis, h0 in spread:
        mine = quarter(axis)
        for slot, step in ((0, 1), (1, -1)):
            send(("z1", h0, slot), ks_ref.at[pl.ds(h0, 2), mine], kbuf.at[slot, pl.ds(h0, 2), mine], near("key", step))

    def key_second():
        for axis, h0 in spread:
            mine = quarter(axis)
            for slot in (0, 1):
                arrived(("z1", h0, slot), kbuf.at[slot, pl.ds(h0, 2), mine])
            for slot, step in ((0, 1), (1, -1)):
                send(("z2", h0, slot), kbuf.at[slot, h0 + slot, mine], kbuf.at[2, h0 + slot, mine], near("key", step))

    def share_first(slot):
        for axis, h0 in spread:
            mine = quarter(axis)
            block = kbuf.at[slot, pl.ds(h0, 2), mine]
            if slot == 2:
                for side in (0, 1):
                    arrived(("z2", h0, side), kbuf.at[2, h0 + side, mine])
            for side, step in ((0, 1), (1, -1)):
                send(("g1", h0, slot, side), block, block, near(axis, step))

    def share_second(slot):
        for axis, h0 in spread:
            for side, step in ((0, 1), (1, -1)):
                theirs = quarter(axis, -step)
                arrived(("g1", h0, slot, side), kbuf.at[slot, pl.ds(h0, 2), theirs])
                half = kbuf.at[slot, h0 + side, theirs]
                send(("g2", h0, slot, side), half, half, near(axis, step))

    def share_end(slot):
        for axis, h0 in spread:
            for side in (0, 1):
                arrived(("g2", h0, slot, side), kbuf.at[slot, h0 + side, quarter(axis, 2)])

    kept, tokens = idx_ref.shape[1], idx_ref.shape[2]
    for hx in range(4):
        idxf[hx] = idx_ref[hx].astype(F32)
    slots = lax.broadcasted_iota(jnp.int32, (kept, tokens), 0)
    for h in range(2):
        product = w_ref[h] * wg_ref[h]
        total = jnp.sum(product, axis=0, keepdims=True)
        score[...] = w_ref[h] * (wg_ref[h] - total)
        first[...] = pair_ref[h] >> 5
        second[...] = pair_ref[h] & 31

        def add_pairs(step, sums):
            one, two = sums
            for sub in range(4):
                row = pl.ds(step * 4 + sub, 1)
                here = score[row, :]
                one = one + jnp.where(slots == first[row, :], here, 0.0)
                two = two + jnp.where(slots == second[row, :], here, 0.0)
            return one, two

        zero = jnp.zeros((kept, tokens), F32)
        one, two = lax.fori_loop(0, kept // 4, add_pairs, (zero, zero))
        val[2 * h] = one
        val[2 * h + 1] = two

    across = 128
    ids = lax.broadcasted_iota(jnp.int32, (16, 16, across), 0) * 16 + lax.broadcasted_iota(jnp.int32, (16, 16, across), 1)
    ids = ids.astype(F32).astype(BF16)

    def build(hx):
        @pl.loop(0, 4)
        def _(b):
            low = (b * 256).astype(F32)
            for lane in range(tokens // across):
                cols = slice(lane * across, (lane + 1) * across)
                acc = jnp.zeros((16, 16, across), BF16)
                for a in range(kept):
                    place = jnp.broadcast_to(idxf[hx, a : a + 1, cols] - low, (16, across)).astype(BF16)
                    value = jnp.broadcast_to(val[hx, a : a + 1, cols], (16, across)).astype(BF16)
                    acc = jnp.where(ids == place[None], value[None], acc)
                table[hx, b, :, cols] = acc.reshape(256, across)
            grad = jnp.dot(table[hx, b], q_ref[hx], preferred_element_type=F32)
            part[hx, b] = grad.astype(BF16).reshape(4, 64, grad.shape[1])

    def way(hx):
        return 1 - 2 * (hx % 2)

    def block(stage, hx, step):
        if stage == 2:
            return res1.at[hx, at("dp_0" if hx < 2 else "dp_1", step)]
        if hx < 2:
            return part.at[hx, :, at("dp_1", step)]
        return part.at[hx, at("dp_0", step)]

    def axis_of(stage, hx):
        return "dp_1" if (hx < 2) == (stage == 1) else "dp_0"

    into = {1: r1, 2: r2}
    staged = {1: s3, 2: s23}

    def reduce_first(stage, hx):
        axis, d = axis_of(stage, hx), way(hx)
        send((stage, hx, 0), block(stage, hx, 2), into[stage].at[hx, 0], near(axis, d))
        send((stage, hx, 1), block(stage, hx, -d), into[stage].at[hx, 1], near(axis, -d))

    def reduce_second(stage, hx):
        axis, d = axis_of(stage, hx), way(hx)
        arrived((stage, hx, 0), into[stage].at[hx, 0])
        both = block(stage, hx, d)[...].astype(F32) + into[stage][hx, 0].astype(F32)
        staged[stage][hx] = both.astype(BF16)
        send((stage, hx, 2), staged[stage].at[hx], into[stage].at[hx, 2], near(axis, d))

    def reduce_end(stage, hx):
        got = into[stage]
        arrived((stage, hx, 1), got.at[hx, 1])
        arrived((stage, hx, 2), got.at[hx, 2])
        total = block(stage, hx, 0)[...].astype(F32) + got[hx, 1].astype(F32) + got[hx, 2].astype(F32)
        if stage == 1:
            res1[hx] = total.astype(BF16)
        else:
            res2[:, hx] = total.astype(BF16).reshape(4, 16, total.shape[-1])

    key_steps = (1, -1, 2)

    build(0)
    reduce_first(1, 0)
    build(1)
    reduce_first(1, 1)
    build(2)
    reduce_first(1, 2)
    key_second()
    share_first(0)
    share_first(1)
    build(3)
    reduce_first(1, 3)
    share_first(2)
    share_second(0)
    share_second(1)
    for hx in range(4):
        reduce_second(1, hx)
    share_second(2)
    for slot in range(3):
        share_end(slot)

    transposed = (((0,), (0,)), ((), ()))
    for hx in range(4):
        total = lax.dot_general(table[hx, k], ks_ref[hx], transposed, preferred_element_type=F32)
        for slot, step in ((0, -1), (1, 1), (2, 2)):
            total += lax.dot_general(table[hx, at("key", step)], kbuf[slot, hx], transposed, preferred_element_type=F32)
        qg[:, hx * 256 : (hx + 1) * 256] = total.astype(BF16)

    def project(j):
        loads[j].wait()
        out = lax.dot_general(qg[...], wv[j * wide : (j + 1) * wide], (((1,), (1,)), ((), ())), preferred_element_type=F32)
        po[j] = out.astype(BF16).reshape(2, 2, 64, wide)
        send(("c1", j), po.at[j, :, 1 - c], c1.at[j], other_core)

    def pass_on(j):
        arrived(("c1", j), c1.at[j])
        c2s[j] = (po[j, 1 - zl, c].astype(F32) + c1[j, 1 - zl].astype(F32)).astype(BF16)
        send(("c2", j), c2s.at[j], c2r.at[j], other_chip)

    for j in range(CHUNKS):
        project(j)
        if j >= 2:
            pass_on(j - 2)
    pass_on(CHUNKS - 2)
    pass_on(CHUNKS - 1)
    for hx in range(4):
        reduce_end(1, hx)
        reduce_first(2, hx)
    for hx in range(4):
        reduce_second(2, hx)
    for hx in range(4):
        reduce_end(2, hx)
    for n, step in enumerate(key_steps):
        send((3, n), res2.at[at("key", step)], r3.at[n], near("key", step))
    for j in range(CHUNKS):
        arrived(("c2", j), c2r.at[j])
        total = po[j, zl, c].astype(F32) + c1[j, zl].astype(F32) + c2r[j].astype(F32)
        in_out[:, j * wide : (j + 1) * wide] = total.astype(BF16)
    total = res2[k].astype(F32)
    for n in range(3):
        arrived((3, n), r3.at[n])
        total = total + r3[n].astype(F32)
    key_out[...] = total
    for one in sent:
        one.wait_send()


def on_device(queries, sub_keys, query_weight, sub_choice, pair_choice, weights, weight_grad):
    tok, heads, halves, width = queries.shape
    topk = pair_choice.shape[2]
    groups = heads * halves
    rows = sub_keys.shape[0]
    model = query_weight.shape[0]
    wide = model // CHUNKS
    idx = jnp.transpose(sub_choice, (1, 2, 3, 0)).reshape(groups, topk, tok)
    pair, w, wg = (jnp.transpose(v, (1, 2, 0)) for v in (pair_choice, weights, weight_grad))
    q = jnp.transpose(queries.reshape(tok, groups, width), (1, 0, 2))
    ks = jnp.transpose(sub_keys.reshape(rows, groups, width), (1, 0, 2))
    vmem = pl.BlockSpec(memory_space=pltpu.VMEM)
    key_grad, in_grad = pl.pallas_call(
        kernel,
        out_shape=(
            jax.ShapeDtypeStruct((groups, 16, width), F32),
            jax.ShapeDtypeStruct((tok // 4, model), BF16),
        ),
        in_specs=[vmem] * 6 + [pl.BlockSpec(memory_space=pl.ANY)],
        out_specs=(vmem, vmem),
        scratch_shapes=[
            pltpu.VMEM((groups, topk, tok), F32),
            pltpu.VMEM((groups, topk, tok), F32),
            pltpu.VMEM((topk, tok), F32),
            pltpu.VMEM((topk, tok), jnp.int32),
            pltpu.VMEM((topk, tok), jnp.int32),
            pltpu.VMEM((groups, 4, rows, tok), BF16),
            pltpu.VMEM((groups, 4, 4, 64, width), BF16),
            pltpu.VMEM((3, groups, rows, width), BF16),
            pltpu.VMEM((model, groups * width), BF16),
            pltpu.VMEM((tok, groups * width), BF16),
            pltpu.VMEM((groups, 3, 4, 64, width), BF16),
            pltpu.VMEM((groups, 4, 64, width), BF16),
            pltpu.VMEM((groups, 4, 64, width), BF16),
            pltpu.VMEM((groups, 3, 64, width), BF16),
            pltpu.VMEM((groups, 64, width), BF16),
            pltpu.VMEM((4, groups, 16, width), BF16),
            pltpu.VMEM((3, groups, 16, width), BF16),
            pltpu.VMEM((CHUNKS, 2, 2, 64, wide), BF16),
            pltpu.VMEM((CHUNKS, 2, 64, wide), BF16),
            pltpu.VMEM((CHUNKS, 64, wide), BF16),
            pltpu.VMEM((CHUNKS, 64, wide), BF16),
            pltpu.SemaphoreType.DMA((CHUNKS,)),
            pltpu.SemaphoreType.DMA((MESSAGES,)),
            pltpu.SemaphoreType.DMA((MESSAGES,)),
        ],
        compiler_params=pltpu.CompilerParams(
            collective_id=0, has_side_effects=True, vmem_limit_bytes=48 * 2**20
        ),
    )(idx, pair, w, wg, q, ks, query_weight)
    sub_key_grad = jnp.transpose(key_grad, (1, 0, 2)).reshape(16, heads, halves, width)
    return sub_key_grad, in_grad


def solution(mesh):
    split = Mesh(
        mesh.devices.reshape(4, 4, mesh.shape["key"], mesh.shape["tensor"]), AXES
    )
    in_specs = (
        P(DP_KEY, "tensor", None, None),
        P("key", "tensor", None, None),
        P(None, "tensor"),
        P(DP_KEY, "tensor", None, None),
        P(DP_KEY, "tensor", None),
        P(DP_KEY, "tensor", None),
        P(DP_KEY, "tensor", None),
    )
    out_specs = (P(DP_KEY, "tensor", None, None), P(DP_KEY_TENSOR, None))
    return jax.shard_map(
        on_device, mesh=split, in_specs=in_specs, out_specs=out_specs, check_vma=False
    )
```

```python
import functools

import jax
import jax.numpy as jnp
from jax import lax
from jax.experimental import pallas as pl
from jax.experimental.pallas import tpu as pltpu
from jax.sharding import Mesh
from jax.sharding import PartitionSpec as P

DP_KEY = ("dp_0", "dp_1", "key")
DP_KEY_TENSOR = ("dp_0", "dp_1", "key", "tensor")
AXES = ("dp_0", "dp_1", "key", "tensor")
MESH = pl.DeviceIdType.MESH
F32 = jnp.float32
BF16 = jnp.bfloat16
CHUNKS = 8
MESSAGES = 96


def kernel(
    idx_hbm, pair_hbm, w_hbm, wg_hbm, q_hbm, ks_hbm, wq_ref,
    key_out, in_out,
    idx_ref, pair_ref, w_ref, wg_ref, q_raw, ks_raw, q_ref, ks_ref,
    idxf, val, score, first, second, table, part, kbuf, wv, qg, qsum,
    r1, s3, res1, r2, s23, res2, r3, po, c1, c2s, c2r,
    w_sem, in_sem, send_sem, recv_sem,
):
    y, x, k, t = (lax.axis_index(a) for a in AXES)
    zl, c = t // 2, lax.rem(t, 2)
    coord = {"dp_0": y, "dp_1": x, "key": k}

    def at(axis, step):
        return lax.rem(coord[axis] + step + 4, 4)

    def near(axis, step):
        return {axis: at(axis, step)}

    other_core = {"tensor": zl * 2 + (1 - c)}
    other_chip = {"tensor": (1 - zl) * 2 + c}

    barrier = pltpu.get_barrier_semaphore()
    partners = [near(a, s) for a in ("dp_0", "dp_1") for s in (1, -1)]
    partners += [near("key", s) for s in (1, -1, 2)] + [other_core, other_chip]
    for device in partners:
        pl.semaphore_signal(barrier, inc=1, device_id=device, device_id_type=MESH)

    fetched = [
        pltpu.make_async_copy(src, dst, in_sem.at[n])
        for n, (src, dst) in enumerate((
            (ks_hbm, ks_raw), (w_hbm, w_ref), (wg_hbm, wg_ref),
            (pair_hbm, pair_ref), (idx_hbm, idx_ref), (q_hbm, q_raw),
        ))
    ]
    for one in fetched:
        one.start()
    wide = wv.shape[0] // CHUNKS
    loads = [
        pltpu.make_async_copy(wq_ref.at[pl.ds(j * wide, wide)], wv.at[pl.ds(j * wide, wide)], w_sem.at[j])
        for j in range(CHUNKS)
    ]
    for load in loads:
        load.start()
    fetched[0].wait()
    for hx in range(4):
        ks_ref[hx] = ks_raw[:, hx // 2, hx % 2, :]
    pl.semaphore_wait(barrier, len(partners))

    names, sent = {}, []

    def copy(name, src, dst, device):
        n = names.setdefault(name, len(names))
        return pltpu.make_async_remote_copy(
            src_ref=src, dst_ref=dst, send_sem=send_sem.at[n], recv_sem=recv_sem.at[n],
            device_id=device, device_id_type=MESH,
        )

    def send(name, src, dst, device):
        one = copy(name, src, dst, device)
        one.start()
        sent.append(one)

    def arrived(name, dst):
        copy(name, dst, dst, other_core).wait_recv()

    def way(hx):
        return 1 - 2 * (hx % 2)

    rows = kbuf.shape[2] // 4

    def ring(hx):
        return "dp_1" if hx < 2 else "dp_0"

    def quarter(hx, step=0):
        return pl.ds(pl.multiple_of(at(ring(hx), step) * rows, rows), rows)

    def key_first(late):
        for hx in range(4):
            d = -way(hx) if late else way(hx)
            slot = (1 - d) // 2
            send(("z1", slot, hx), ks_ref.at[hx, quarter(hx)], kbuf.at[slot, hx, quarter(hx)], near("key", d))

    def key_second():
        for hx in range(4):
            d = way(hx)
            slot = (1 - d) // 2
            piece = kbuf.at[slot, hx, quarter(hx)]
            arrived(("z1", slot, hx), piece)
            send(("z2", hx), piece, kbuf.at[2, hx, quarter(hx)], near("key", d))

    def share_first(slot, hx, name=None):
        piece = kbuf.at[slot, hx, quarter(hx)]
        if name is not None:
            arrived(name, piece)
        for d in (way(hx), -way(hx)):
            send(("g1", slot, hx, d), piece, piece, near(ring(hx), d))

    def share_second(slot, hx):
        d = way(hx)
        piece = kbuf.at[slot, hx, quarter(hx, -d)]
        arrived(("g1", slot, hx, d), piece)
        send(("g2", slot, hx), piece, piece, near(ring(hx), d))

    def share_end(slot):
        for hx in range(4):
            d = way(hx)
            arrived(("g1", slot, hx, -d), kbuf.at[slot, hx, quarter(hx, d)])
            arrived(("g2", slot, hx), kbuf.at[slot, hx, quarter(hx, 2)])

    def early(hx):
        return (1 - way(hx)) // 2

    key_first(False)
    key_first(True)

    for one in fetched[1:]:
        one.wait()
    for hx in range(4):
        q_ref[hx] = q_raw[:, hx // 2, hx % 2, :]

    kept, tokens = idx_ref.shape[1], idx_ref.shape[2]
    for hx in range(4):
        idxf[hx] = idx_ref[hx].astype(F32)
    slots = lax.broadcasted_iota(jnp.int32, (kept, tokens), 0)
    for h in range(2):
        product = w_ref[h] * wg_ref[h]
        total = jnp.sum(product, axis=0, keepdims=True)
        score[...] = w_ref[h] * (wg_ref[h] - total)
        first[...] = pair_ref[h] >> 5
        second[...] = pair_ref[h] & 31

        def add_pairs(step, sums):
            one, two = sums
            for sub in range(4):
                row = pl.ds(step * 4 + sub, 1)
                here = score[row, :]
                one = one + jnp.where(slots == first[row, :], here, 0.0)
                two = two + jnp.where(slots == second[row, :], here, 0.0)
            return one, two

        zero = jnp.zeros((kept, tokens), F32)
        one, two = lax.fori_loop(0, kept // 4, add_pairs, (zero, zero))
        val[2 * h] = one
        val[2 * h + 1] = two

    across = 128
    ids = lax.broadcasted_iota(jnp.int32, (16, 16, across), 0) * 16 + lax.broadcasted_iota(jnp.int32, (16, 16, across), 1)
    ids = ids.astype(F32).astype(BF16)

    def build(hx):
        @pl.loop(0, 4)
        def _(b):
            low = (b * 256).astype(F32)
            for lane in range(tokens // across):
                cols = slice(lane * across, (lane + 1) * across)
                acc = jnp.zeros((16, 16, across), BF16)
                for a in range(kept):
                    place = jnp.broadcast_to(idxf[hx, a : a + 1, cols] - low, (16, across)).astype(BF16)
                    value = jnp.broadcast_to(val[hx, a : a + 1, cols], (16, across)).astype(BF16)
                    acc = jnp.where(ids == place[None], value[None], acc)
                table[hx, b, :, cols] = acc.reshape(256, across)
            grad = jnp.dot(table[hx, b], q_ref[hx], preferred_element_type=F32)
            part[hx, b] = grad.astype(BF16).reshape(4, 64, grad.shape[1])

    def block(stage, hx, step):
        if stage == 2:
            return res1.at[hx, at("dp_0" if hx < 2 else "dp_1", step)]
        if hx < 2:
            return part.at[hx, :, at("dp_1", step)]
        return part.at[hx, at("dp_0", step)]

    def axis_of(stage, hx):
        return "dp_1" if (hx < 2) == (stage == 1) else "dp_0"

    into = {1: r1, 2: r2}
    staged = {1: s3, 2: s23}

    def reduce_first(stage, hx):
        axis, d = axis_of(stage, hx), way(hx)
        send((stage, hx, 0), block(stage, hx, 2), into[stage].at[hx, 0], near(axis, d))
        send((stage, hx, 1), block(stage, hx, -d), into[stage].at[hx, 1], near(axis, -d))

    def reduce_second(stage, hx):
        axis, d = axis_of(stage, hx), way(hx)
        arrived((stage, hx, 0), into[stage].at[hx, 0])
        both = block(stage, hx, d)[...].astype(F32) + into[stage][hx, 0].astype(F32)
        staged[stage][hx] = both.astype(BF16)
        send((stage, hx, 2), staged[stage].at[hx], into[stage].at[hx, 2], near(axis, d))

    def reduce_end(stage, hx):
        got = into[stage]
        arrived((stage, hx, 1), got.at[hx, 1])
        arrived((stage, hx, 2), got.at[hx, 2])
        total = block(stage, hx, 0)[...].astype(F32) + got[hx, 1].astype(F32) + got[hx, 2].astype(F32)
        if stage == 1:
            res1[hx] = total.astype(BF16)
        else:
            res2[:, hx] = total.astype(BF16).reshape(4, 16, total.shape[-1])

    key_steps = (1, -1, 2)

    build(0)
    reduce_first(1, 0)
    key_second()
    for hx in range(4):
        share_first(early(hx), hx)
    build(2)
    reduce_first(1, 2)
    for hx in range(4):
        share_first(1 - early(hx), hx, ("z1", 1 - early(hx), hx))
    build(1)
    reduce_first(1, 1)
    for hx in range(4):
        share_second(early(hx), hx)
    for hx in (0, 2):
        reduce_second(1, hx)
    for hx in range(4):
        share_first(2, hx, ("z2", hx))
    for hx in range(4):
        share_second(1 - early(hx), hx)
    build(3)
    reduce_first(1, 3)
    for hx in range(4):
        share_second(2, hx)
    share_end(0)
    share_end(1)

    transposed = (((0,), (0,)), ((), ()))

    def shard_term(hx, step, shard):
        return lax.dot_general(table[hx, at("key", step)], shard, transposed, preferred_element_type=F32)

    for hx in range(4):
        qsum[hx] = shard_term(hx, 0, ks_ref[hx]) + shard_term(hx, -1, kbuf[0, hx]) + shard_term(hx, 1, kbuf[1, hx])
    reduce_second(1, 1)
    share_end(2)
    for hx in range(4):
        total = qsum[hx] + shard_term(hx, 2, kbuf[2, hx])
        qg[:, hx * 256 : (hx + 1) * 256] = total.astype(BF16)

    def project(j):
        loads[j].wait()
        out = lax.dot_general(qg[...], wv[j * wide : (j + 1) * wide], (((1,), (1,)), ((), ())), preferred_element_type=F32)
        po[j] = out.astype(BF16).reshape(2, 2, 64, wide)
        send(("c1", j), po.at[j, :, 1 - c], c1.at[j], other_core)

    def pass_on(j):
        arrived(("c1", j), c1.at[j])
        c2s[j] = (po[j, 1 - zl, c].astype(F32) + c1[j, 1 - zl].astype(F32)).astype(BF16)
        send(("c2", j), c2s.at[j], c2r.at[j], other_chip)

    for j in range(CHUNKS):
        project(j)
        if j >= 2:
            pass_on(j - 2)
        if j == 2:
            reduce_second(1, 3)
        if j >= CHUNKS - 4:
            hx = (0, 2, 1, 3)[j - CHUNKS + 4]
            reduce_end(1, hx)
            reduce_first(2, hx)
    pass_on(CHUNKS - 2)
    pass_on(CHUNKS - 1)
    for hx in (0, 2, 1, 3):
        reduce_second(2, hx)
    for hx in (0, 2, 1, 3):
        reduce_end(2, hx)
    for n, step in enumerate(key_steps):
        send((3, n), res2.at[at("key", step)], r3.at[n], near("key", step))
    for j in range(CHUNKS):
        arrived(("c2", j), c2r.at[j])
        total = po[j, zl, c].astype(F32) + c1[j, zl].astype(F32) + c2r[j].astype(F32)
        in_out[:, j * wide : (j + 1) * wide] = total.astype(BF16)
    total = res2[k].astype(F32)
    for n in range(3):
        arrived((3, n), r3.at[n])
        total = total + r3[n].astype(F32)
    key_out[...] = total
    for one in sent:
        one.wait_send()


def on_device(queries, sub_keys, query_weight, sub_choice, pair_choice, weights, weight_grad):
    tok, heads, halves, width = queries.shape
    topk = pair_choice.shape[2]
    groups = heads * halves
    rows = sub_keys.shape[0]
    model = query_weight.shape[0]
    wide = model // CHUNKS
    idx = jnp.transpose(sub_choice, (1, 2, 3, 0)).reshape(groups, topk, tok)
    pair, w, wg = (jnp.transpose(v, (1, 2, 0)) for v in (pair_choice, weights, weight_grad))
    vmem = pl.BlockSpec(memory_space=pltpu.VMEM)
    key_grad, in_grad = pl.pallas_call(
        kernel,
        out_shape=(
            jax.ShapeDtypeStruct((groups, 16, width), F32),
            jax.ShapeDtypeStruct((tok // 4, model), BF16),
        ),
        in_specs=[pl.BlockSpec(memory_space=pltpu.HBM)] * 7,
        out_specs=(vmem, vmem),
        scratch_shapes=[
            pltpu.VMEM(idx.shape, idx.dtype),
            pltpu.VMEM(pair.shape, pair.dtype),
            pltpu.VMEM(w.shape, w.dtype),
            pltpu.VMEM(wg.shape, wg.dtype),
            pltpu.VMEM(queries.shape, queries.dtype),
            pltpu.VMEM(sub_keys.shape, sub_keys.dtype),
            pltpu.VMEM((groups, tok, width), queries.dtype),
            pltpu.VMEM((groups, rows, width), sub_keys.dtype),
            pltpu.VMEM((groups, topk, tok), F32),
            pltpu.VMEM((groups, topk, tok), F32),
            pltpu.VMEM((topk, tok), F32),
            pltpu.VMEM((topk, tok), jnp.int32),
            pltpu.VMEM((topk, tok), jnp.int32),
            pltpu.VMEM((groups, 4, rows, tok), BF16),
            pltpu.VMEM((groups, 4, 4, 64, width), BF16),
            pltpu.VMEM((3, groups, rows, width), BF16),
            pltpu.VMEM((model, groups * width), BF16),
            pltpu.VMEM((tok, groups * width), BF16),
            pltpu.VMEM((groups, tok, width), F32),
            pltpu.VMEM((groups, 3, 4, 64, width), BF16),
            pltpu.VMEM((groups, 4, 64, width), BF16),
            pltpu.VMEM((groups, 4, 64, width), BF16),
            pltpu.VMEM((groups, 3, 64, width), BF16),
            pltpu.VMEM((groups, 64, width), BF16),
            pltpu.VMEM((4, groups, 16, width), BF16),
            pltpu.VMEM((3, groups, 16, width), BF16),
            pltpu.VMEM((CHUNKS, 2, 2, 64, wide), BF16),
            pltpu.VMEM((CHUNKS, 2, 64, wide), BF16),
            pltpu.VMEM((CHUNKS, 64, wide), BF16),
            pltpu.VMEM((CHUNKS, 64, wide), BF16),
            pltpu.SemaphoreType.DMA((CHUNKS,)),
            pltpu.SemaphoreType.DMA((6,)),
            pltpu.SemaphoreType.DMA((MESSAGES,)),
            pltpu.SemaphoreType.DMA((MESSAGES,)),
        ],
        compiler_params=pltpu.CompilerParams(
            collective_id=0, has_side_effects=True, vmem_limit_bytes=48 * 2**20
        ),
    )(idx, pair, w, wg, queries, sub_keys, query_weight)
    sub_key_grad = jnp.transpose(key_grad, (1, 0, 2)).reshape(16, heads, halves, width)
    return sub_key_grad, in_grad


def solution(mesh):
    split = Mesh(
        mesh.devices.reshape(4, 4, mesh.shape["key"], mesh.shape["tensor"]), AXES
    )
    in_specs = (
        P(DP_KEY, "tensor", None, None),
        P("key", "tensor", None, None),
        P(None, "tensor"),
        P(DP_KEY, "tensor", None, None),
        P(DP_KEY, "tensor", None),
        P(DP_KEY, "tensor", None),
        P(DP_KEY, "tensor", None),
    )
    out_specs = (P(DP_KEY, "tensor", None, None), P(DP_KEY_TENSOR, None))
    return jax.shard_map(
        on_device, mesh=split, in_specs=in_specs, out_specs=out_specs, check_vma=False
    )
```

```python
import functools

import jax
import jax.numpy as jnp
from jax import lax
from jax.experimental import pallas as pl
from jax.experimental.pallas import tpu as pltpu
from jax.sharding import Mesh
from jax.sharding import PartitionSpec as P

DP_KEY = ("dp_0", "dp_1", "key")
DP_KEY_TENSOR = ("dp_0", "dp_1", "key", "tensor")
AXES = ("dp_0", "dp_1", "key", "tensor")
MESH = pl.DeviceIdType.MESH
F32 = jnp.float32
BF16 = jnp.bfloat16
CHUNKS = 8
OTHERS = (2, 1, -1)
MESSAGES = 96


def kernel(
    idx_hbm, pair_hbm, w_hbm, wg_hbm, q_hbm, ks_hbm, wq_ref,
    key_out, in_out,
    idx_ref, pair_ref, w_ref, wg_ref, q_raw, ks_raw, q_ref, ks_ref,
    idxf, val, score, first, second, table, part, kbuf, wv, qg, qsum,
    r1, s3, res1, r2, res2, r3, po, c1, c2s, c2r,
    w_sem, in_sem, send_sem, recv_sem,
):
    y, x, k, t = (lax.axis_index(a) for a in AXES)
    zl, c = t // 2, lax.rem(t, 2)
    coord = {"dp_0": y, "dp_1": x, "key": k}

    def at(axis, step):
        return lax.rem(coord[axis] + step + 4, 4)

    def near(axis, step):
        return {axis: at(axis, step)}

    other_core = {"tensor": zl * 2 + (1 - c)}
    other_chip = {"tensor": (1 - zl) * 2 + c}

    barrier = pltpu.get_barrier_semaphore()
    partners = [near(a, s) for a in ("dp_0", "dp_1") for s in OTHERS]
    partners += [near("key", s) for s in OTHERS] + [other_core, other_chip]
    for device in partners:
        pl.semaphore_signal(barrier, inc=1, device_id=device, device_id_type=MESH)

    fetched = [
        pltpu.make_async_copy(src, dst, in_sem.at[n])
        for n, (src, dst) in enumerate((
            (ks_hbm, ks_raw), (w_hbm, w_ref), (wg_hbm, wg_ref),
            (pair_hbm, pair_ref), (idx_hbm, idx_ref), (q_hbm, q_raw),
        ))
    ]
    for one in fetched:
        one.start()
    wide = wv.shape[0] // CHUNKS
    loads = [
        pltpu.make_async_copy(wq_ref.at[pl.ds(j * wide, wide)], wv.at[pl.ds(j * wide, wide)], w_sem.at[j])
        for j in range(CHUNKS)
    ]
    for load in loads:
        load.start()
    fetched[0].wait()
    for hx in range(4):
        ks_ref[hx] = ks_raw[:, hx // 2, hx % 2, :]
    pl.semaphore_wait(barrier, len(partners))

    names, sent = {}, []

    def copy(name, src, dst, device):
        n = names.setdefault(name, len(names))
        return pltpu.make_async_remote_copy(
            src_ref=src, dst_ref=dst, send_sem=send_sem.at[n], recv_sem=recv_sem.at[n],
            device_id=device, device_id_type=MESH,
        )

    def send(name, src, dst, device):
        one = copy(name, src, dst, device)
        one.start()
        sent.append(one)

    def arrived(name, dst):
        copy(name, dst, dst, other_core).wait_recv()

    def way(hx):
        return 1 - 2 * (hx % 2)

    rows = kbuf.shape[2] // 4

    def ring(hx):
        return "dp_1" if hx < 2 else "dp_0"

    def quarter(hx, step=0):
        return pl.ds(pl.multiple_of(at(ring(hx), step) * rows, rows), rows)

    def key_first(late):
        for hx in range(4):
            d = -way(hx) if late else way(hx)
            slot = (1 - d) // 2
            send(("z1", slot, hx), ks_ref.at[hx, quarter(hx)], kbuf.at[slot, hx, quarter(hx)], near("key", d))

    def key_second():
        for hx in range(4):
            d = way(hx)
            slot = (1 - d) // 2
            piece = kbuf.at[slot, hx, quarter(hx)]
            arrived(("z1", slot, hx), piece)
            send(("z2", hx), piece, kbuf.at[2, hx, quarter(hx)], near("key", d))

    def share(slot, hx, name=None):
        piece = kbuf.at[slot, hx, quarter(hx)]
        if name is not None:
            arrived(name, piece)
        for step in OTHERS:
            send(("g", slot, hx, step), piece, piece, near(ring(hx), step))

    def share_end(slot):
        for hx in range(4):
            for step in OTHERS:
                arrived(("g", slot, hx, step), kbuf.at[slot, hx, quarter(hx, -step)])

    def early(hx):
        return (1 - way(hx)) // 2

    key_first(False)
    key_first(True)

    for one in fetched[1:]:
        one.wait()
    for hx in range(4):
        q_ref[hx] = q_raw[:, hx // 2, hx % 2, :]

    kept, tokens = idx_ref.shape[1], idx_ref.shape[2]
    for hx in range(4):
        idxf[hx] = idx_ref[hx].astype(F32)
    slots = lax.broadcasted_iota(jnp.int32, (kept, tokens), 0)
    for h in range(2):
        product = w_ref[h] * wg_ref[h]
        total = jnp.sum(product, axis=0, keepdims=True)
        score[...] = w_ref[h] * (wg_ref[h] - total)
        first[...] = pair_ref[h] >> 5
        second[...] = pair_ref[h] & 31

        def add_pairs(step, sums):
            one, two = sums
            for sub in range(4):
                row = pl.ds(step * 4 + sub, 1)
                here = score[row, :]
                one = one + jnp.where(slots == first[row, :], here, 0.0)
                two = two + jnp.where(slots == second[row, :], here, 0.0)
            return one, two

        zero = jnp.zeros((kept, tokens), F32)
        one, two = lax.fori_loop(0, kept // 4, add_pairs, (zero, zero))
        val[2 * h] = one
        val[2 * h + 1] = two

    across = 128
    ids = lax.broadcasted_iota(jnp.int32, (16, 16, across), 0) * 16 + lax.broadcasted_iota(jnp.int32, (16, 16, across), 1)
    ids = ids.astype(F32).astype(BF16)

    def build(hx):
        @pl.loop(0, 4)
        def _(b):
            low = (b * 256).astype(F32)
            for lane in range(tokens // across):
                cols = slice(lane * across, (lane + 1) * across)
                acc = jnp.zeros((16, 16, across), BF16)
                for a in range(kept):
                    place = jnp.broadcast_to(idxf[hx, a : a + 1, cols] - low, (16, across)).astype(BF16)
                    value = jnp.broadcast_to(val[hx, a : a + 1, cols], (16, across)).astype(BF16)
                    acc = jnp.where(ids == place[None], value[None], acc)
                table[hx, b, :, cols] = acc.reshape(256, across)
            grad = jnp.dot(table[hx, b], q_ref[hx], preferred_element_type=F32)
            part[hx, b] = grad.astype(BF16).reshape(4, 64, grad.shape[1])

    def block(stage, hx, step):
        if stage == 2:
            return res1.at[hx, at("dp_0" if hx < 2 else "dp_1", step)]
        if hx < 2:
            return part.at[hx, :, at("dp_1", step)]
        return part.at[hx, at("dp_0", step)]

    def axis_of(stage, hx):
        return "dp_1" if (hx < 2) == (stage == 1) else "dp_0"

    into = {1: r1, 2: r2}

    def relayed(stage, hx):
        return stage == 1 and hx % 2 == 0

    def reduce_first(stage, hx):
        axis, got = axis_of(stage, hx), into[stage]
        if relayed(stage, hx):
            send((stage, hx, 0), block(stage, hx, 2), got.at[hx, 0], near(axis, 1))
            send((stage, hx, 2), block(stage, hx, -1), got.at[hx, 2], near(axis, -1))
        else:
            for n, step in enumerate(OTHERS):
                send((stage, hx, n), block(stage, hx, step), got.at[hx, n], near(axis, step))

    def reduce_second(stage, hx):
        axis, got = axis_of(stage, hx), into[stage]
        arrived((stage, hx, 0), got.at[hx, 0])
        both = block(stage, hx, 1)[...].astype(F32) + got[hx, 0].astype(F32)
        s3[hx] = both.astype(BF16)
        send((stage, hx, 1), s3.at[hx], got.at[hx, 1], near(axis, 1))

    def reduce_end(stage, hx):
        got = into[stage]
        total = block(stage, hx, 0)[...].astype(F32)
        for n in range(1 if relayed(stage, hx) else 0, 3):
            arrived((stage, hx, n), got.at[hx, n])
            total = total + got[hx, n].astype(F32)
        if stage == 1:
            res1[hx] = total.astype(BF16)
        else:
            res2[:, hx] = total.astype(BF16).reshape(4, 16, total.shape[-1])

    build(0)
    reduce_first(1, 0)
    key_second()
    for hx in range(4):
        share(early(hx), hx)
    build(2)
    reduce_first(1, 2)
    for hx in range(4):
        share(1 - early(hx), hx, ("z1", 1 - early(hx), hx))
    build(1)
    reduce_second(1, 0)
    for hx in range(4):
        share(2, hx, ("z2", hx))
    reduce_first(1, 1)
    build(3)
    reduce_second(1, 2)
    reduce_first(1, 3)
    share_end(0)
    share_end(1)

    transposed = (((0,), (0,)), ((), ()))

    def shard_term(hx, step, shard):
        return lax.dot_general(table[hx, at("key", step)], shard, transposed, preferred_element_type=F32)

    for hx in range(4):
        qsum[hx] = shard_term(hx, 0, ks_ref[hx]) + shard_term(hx, -1, kbuf[0, hx]) + shard_term(hx, 1, kbuf[1, hx])
    share_end(2)
    for hx in range(4):
        total = qsum[hx] + shard_term(hx, 2, kbuf[2, hx])
        qg[:, hx * 256 : (hx + 1) * 256] = total.astype(BF16)

    def project(j):
        loads[j].wait()
        out = lax.dot_general(qg[...], wv[j * wide : (j + 1) * wide], (((1,), (1,)), ((), ())), preferred_element_type=F32)
        po[j] = out.astype(BF16).reshape(2, 2, 64, wide)
        send(("c1", j), po.at[j, :, 1 - c], c1.at[j], other_core)

    def pass_on(j):
        arrived(("c1", j), c1.at[j])
        c2s[j] = (po[j, 1 - zl, c].astype(F32) + c1[j, 1 - zl].astype(F32)).astype(BF16)
        send(("c2", j), c2s.at[j], c2r.at[j], other_chip)

    def finish(j):
        arrived(("c2", j), c2r.at[j])
        total = po[j, zl, c].astype(F32) + c1[j, zl].astype(F32) + c2r[j].astype(F32)
        in_out[:, j * wide : (j + 1) * wide] = total.astype(BF16)

    held = 2
    for j in range(CHUNKS):
        project(j)
        if j >= 2:
            pass_on(j - 2)
        if j in (2, 3):
            reduce_end(1, 2 * j - 4)
            reduce_first(2, 2 * j - 4)
    for hx in (1, 3):
        reduce_end(1, hx)
        reduce_first(2, hx)
    for j in range(2):
        finish(j)
    for hx in (0, 2, 1, 3):
        reduce_end(2, hx)
    for n, step in enumerate(OTHERS):
        send((3, n), res2.at[at("key", step)], r3.at[n], near("key", step))
    for j in range(CHUNKS - held, CHUNKS):
        pass_on(j)
    for j in range(2, CHUNKS):
        finish(j)
    total = res2[k].astype(F32)
    for n in range(3):
        arrived((3, n), r3.at[n])
        total = total + r3[n].astype(F32)
    key_out[...] = total
    for one in sent:
        one.wait_send()


def on_device(queries, sub_keys, query_weight, sub_choice, pair_choice, weights, weight_grad):
    tok, heads, halves, width = queries.shape
    topk = pair_choice.shape[2]
    groups = heads * halves
    rows = sub_keys.shape[0]
    model = query_weight.shape[0]
    wide = model // CHUNKS
    idx = jnp.transpose(sub_choice, (1, 2, 3, 0)).reshape(groups, topk, tok)
    pair, w, wg = (jnp.transpose(v, (1, 2, 0)) for v in (pair_choice, weights, weight_grad))
    vmem = pl.BlockSpec(memory_space=pltpu.VMEM)
    key_grad, in_grad = pl.pallas_call(
        kernel,
        out_shape=(
            jax.ShapeDtypeStruct((groups, 16, width), F32),
            jax.ShapeDtypeStruct((tok // 4, model), BF16),
        ),
        in_specs=[pl.BlockSpec(memory_space=pltpu.HBM)] * 7,
        out_specs=(vmem, vmem),
        scratch_shapes=[
            pltpu.VMEM(idx.shape, idx.dtype),
            pltpu.VMEM(pair.shape, pair.dtype),
            pltpu.VMEM(w.shape, w.dtype),
            pltpu.VMEM(wg.shape, wg.dtype),
            pltpu.VMEM(queries.shape, queries.dtype),
            pltpu.VMEM(sub_keys.shape, sub_keys.dtype),
            pltpu.VMEM((groups, tok, width), queries.dtype),
            pltpu.VMEM((groups, rows, width), sub_keys.dtype),
            pltpu.VMEM((groups, topk, tok), F32),
            pltpu.VMEM((groups, topk, tok), F32),
            pltpu.VMEM((topk, tok), F32),
            pltpu.VMEM((topk, tok), jnp.int32),
            pltpu.VMEM((topk, tok), jnp.int32),
            pltpu.VMEM((groups, 4, rows, tok), BF16),
            pltpu.VMEM((groups, 4, 4, 64, width), BF16),
            pltpu.VMEM((3, groups, rows, width), BF16),
            pltpu.VMEM((model, groups * width), BF16),
            pltpu.VMEM((tok, groups * width), BF16),
            pltpu.VMEM((groups, tok, width), F32),
            pltpu.VMEM((groups, 3, 4, 64, width), BF16),
            pltpu.VMEM((groups, 4, 64, width), BF16),
            pltpu.VMEM((groups, 4, 64, width), BF16),
            pltpu.VMEM((groups, 3, 64, width), BF16),
            pltpu.VMEM((4, groups, 16, width), BF16),
            pltpu.VMEM((3, groups, 16, width), BF16),
            pltpu.VMEM((CHUNKS, 2, 2, 64, wide), BF16),
            pltpu.VMEM((CHUNKS, 2, 64, wide), BF16),
            pltpu.VMEM((CHUNKS, 64, wide), BF16),
            pltpu.VMEM((CHUNKS, 64, wide), BF16),
            pltpu.SemaphoreType.DMA((CHUNKS,)),
            pltpu.SemaphoreType.DMA((6,)),
            pltpu.SemaphoreType.DMA((MESSAGES,)),
            pltpu.SemaphoreType.DMA((MESSAGES,)),
        ],
        compiler_params=pltpu.CompilerParams(
            collective_id=0, has_side_effects=True, vmem_limit_bytes=40000000
        ),
    )(*(pltpu.with_memory_space_constraint(v, pltpu.HBM) for v in (idx, pair, w, wg, queries, sub_keys, query_weight)))
    sub_key_grad = jnp.transpose(key_grad, (1, 0, 2)).reshape(16, heads, halves, width)
    return sub_key_grad, in_grad


def solution(mesh):
    split = Mesh(
        mesh.devices.reshape(4, 4, mesh.shape["key"], mesh.shape["tensor"]), AXES
    )
    in_specs = (
        P(DP_KEY, "tensor", None, None),
        P("key", "tensor", None, None),
        P(None, "tensor"),
        P(DP_KEY, "tensor", None, None),
        P(DP_KEY, "tensor", None),
        P(DP_KEY, "tensor", None),
        P(DP_KEY, "tensor", None),
    )
    out_specs = (P(DP_KEY, "tensor", None, None), P(DP_KEY_TENSOR, None))
    return jax.shard_map(
        on_device, mesh=split, in_specs=in_specs, out_specs=out_specs, check_vma=False
    )
```

```python
import functools

import jax
import jax.numpy as jnp
from jax import lax
from jax.experimental import pallas as pl
from jax.experimental.pallas import tpu as pltpu
from jax.sharding import Mesh
from jax.sharding import PartitionSpec as P

DP_KEY = ("dp_0", "dp_1", "key")
DP_KEY_TENSOR = ("dp_0", "dp_1", "key", "tensor")
AXES = ("dp_0", "dp_1", "key", "tensor")
MESH = pl.DeviceIdType.MESH
F32 = jnp.float32
BF16 = jnp.bfloat16
CHUNKS = 8
OTHERS = (2, 1, -1)
MESSAGES = 96


def kernel(
    idx_hbm, pair_hbm, w_hbm, wg_hbm, q_hbm, ks_hbm, wq_ref,
    key_out, in_out,
    idx_ref, pair_ref, w_ref, wg_ref, q_raw, ks_raw, pairs, q_ref, ks_ref,
    idxf, val, score, first, second, table, part, kbuf, wv, qg, qsum,
    r1, s3, res1, r2, res2, r3, po, c1, c2s, c2r,
    w_sem, in_sem, send_sem, recv_sem,
):
    y, x, k, t = (lax.axis_index(a) for a in AXES)
    zl, c = t // 2, lax.rem(t, 2)
    coord = {"dp_0": y, "dp_1": x, "key": k}

    def at(axis, step):
        return lax.rem(coord[axis] + step + 4, 4)

    def near(axis, step):
        return {axis: at(axis, step)}

    other_core = {"tensor": zl * 2 + (1 - c)}
    other_chip = {"tensor": (1 - zl) * 2 + c}

    barrier = pltpu.get_barrier_semaphore()
    partners = [near(a, s) for a in ("dp_0", "dp_1") for s in OTHERS]
    partners += [near("key", s) for s in OTHERS] + [other_core, other_chip]
    for device in partners:
        pl.semaphore_signal(barrier, inc=1, device_id=device, device_id_type=MESH)

    fetched = [
        pltpu.make_async_copy(src, dst, in_sem.at[n])
        for n, (src, dst) in enumerate((
            (ks_hbm, ks_raw), (w_hbm, w_ref), (wg_hbm, wg_ref),
            (pair_hbm, pair_ref), (idx_hbm, idx_ref), (q_hbm, q_raw),
        ))
    ]
    for one in fetched:
        one.start()
    wide = wv.shape[0] // CHUNKS
    loads = [
        pltpu.make_async_copy(wq_ref.at[pl.ds(j * wide, wide)], wv.at[pl.ds(j * wide, wide)], w_sem.at[j])
        for j in range(CHUNKS)
    ]
    for load in loads:
        load.start()
    fetched[0].wait()

    def lay_out(raw, dst):
        for h in range(2):
            both = raw[:, h].astype(F32).reshape(2 * raw.shape[0], raw.shape[3])
            for n in range(raw.shape[3] // 128):
                lanes = slice(n * 128, (n + 1) * 128)
                pairs[n] = both[:, lanes]
                for half in range(2):
                    dst[2 * h + half, :, lanes] = pairs[n, pl.ds(half, raw.shape[0], stride=2), :].astype(BF16)

    lay_out(ks_raw, ks_ref)
    pl.semaphore_wait(barrier, len(partners))

    names, sent = {}, []

    def copy(name, src, dst, device):
        n = names.setdefault(name, len(names))
        return pltpu.make_async_remote_copy(
            src_ref=src, dst_ref=dst, send_sem=send_sem.at[n], recv_sem=recv_sem.at[n],
            device_id=device, device_id_type=MESH,
        )

    def send(name, src, dst, device):
        one = copy(name, src, dst, device)
        one.start()
        sent.append(one)

    def arrived(name, dst):
        copy(name, dst, dst, other_core).wait_recv()

    def way(hx):
        return 1 - 2 * (hx % 2)

    rows = kbuf.shape[2] // 4

    def ring(hx):
        return "dp_1" if hx < 2 else "dp_0"

    def quarter(hx, step=0):
        return pl.ds(pl.multiple_of(at(ring(hx), step) * rows, rows), rows)

    def key_first(late):
        for hx in range(4):
            d = -way(hx) if late else way(hx)
            slot = (1 - d) // 2
            send(("z1", slot, hx), ks_ref.at[hx, quarter(hx)], kbuf.at[slot, hx, quarter(hx)], near("key", d))

    def key_second():
        for hx in range(4):
            d = way(hx)
            slot = (1 - d) // 2
            piece = kbuf.at[slot, hx, quarter(hx)]
            arrived(("z1", slot, hx), piece)
            send(("z2", hx), piece, kbuf.at[2, hx, quarter(hx)], near("key", d))

    def share(slot, hx, name=None):
        piece = kbuf.at[slot, hx, quarter(hx)]
        if name is not None:
            arrived(name, piece)
        for step in OTHERS:
            send(("g", slot, hx, step), piece, piece, near(ring(hx), step))

    def share_end(slot):
        for hx in range(4):
            for step in OTHERS:
                arrived(("g", slot, hx, step), kbuf.at[slot, hx, quarter(hx, -step)])

    def early(hx):
        return (1 - way(hx)) // 2

    key_first(False)
    key_first(True)

    for one in fetched[1:]:
        one.wait()
    lay_out(q_raw, q_ref)

    kept, tokens = idx_ref.shape[1], idx_ref.shape[2]
    for hx in range(4):
        idxf[hx] = idx_ref[hx].astype(F32)
    slots = lax.broadcasted_iota(jnp.int32, (kept, tokens), 0)
    for h in range(2):
        product = w_ref[h] * wg_ref[h]
        total = jnp.sum(product, axis=0, keepdims=True)
        score[...] = w_ref[h] * (wg_ref[h] - total)
        first[...] = pair_ref[h] >> 5
        second[...] = pair_ref[h] & 31

        def add_pairs(step, sums):
            one, two = sums
            for sub in range(4):
                row = pl.ds(step * 4 + sub, 1)
                here = score[row, :]
                one = one + jnp.where(slots == first[row, :], here, 0.0)
                two = two + jnp.where(slots == second[row, :], here, 0.0)
            return one, two

        zero = jnp.zeros((kept, tokens), F32)
        one, two = lax.fori_loop(0, kept // 4, add_pairs, (zero, zero))
        val[2 * h] = one
        val[2 * h + 1] = two

    across = 128
    ids = lax.broadcasted_iota(jnp.int32, (16, 16, across), 0) * 16 + lax.broadcasted_iota(jnp.int32, (16, 16, across), 1)
    ids = ids.astype(F32).astype(BF16)

    def build(hx):
        @pl.loop(0, 4)
        def _(b):
            low = (b * 256).astype(F32)
            for lane in range(tokens // across):
                cols = slice(lane * across, (lane + 1) * across)
                acc = jnp.zeros((16, 16, across), BF16)
                for a in range(kept):
                    place = jnp.broadcast_to(idxf[hx, a : a + 1, cols] - low, (16, across)).astype(BF16)
                    value = jnp.broadcast_to(val[hx, a : a + 1, cols], (16, across)).astype(BF16)
                    acc = jnp.where(ids == place[None], value[None], acc)
                table[hx, b, :, cols] = acc.reshape(256, across)
            grad = jnp.dot(table[hx, b], q_ref[hx], preferred_element_type=F32)
            part[hx, b] = grad.astype(BF16).reshape(4, 64, grad.shape[1])

    def block(stage, hx, step):
        if stage == 2:
            return res1.at[hx, at("dp_0" if hx < 2 else "dp_1", step)]
        if hx < 2:
            return part.at[hx, :, at("dp_1", step)]
        return part.at[hx, at("dp_0", step)]

    def axis_of(stage, hx):
        return "dp_1" if (hx < 2) == (stage == 1) else "dp_0"

    into = {1: r1, 2: r2}
    lean = 1 - 2 * c

    def relayed(stage, hx):
        return stage == 1 and hx % 2 == 0

    def reduce_first(stage, hx):
        axis, got = axis_of(stage, hx), into[stage]
        if relayed(stage, hx):
            send((stage, hx, 0), block(stage, hx, 2), got.at[hx, 0], near(axis, lean))
            send((stage, hx, 2), block(stage, hx, -lean), got.at[hx, 2], near(axis, -lean))
        else:
            for n, step in enumerate(OTHERS):
                send((stage, hx, n), block(stage, hx, step), got.at[hx, n], near(axis, step))

    def reduce_second(stage, hx):
        axis, got = axis_of(stage, hx), into[stage]
        arrived((stage, hx, 0), got.at[hx, 0])
        both = block(stage, hx, lean)[...].astype(F32) + got[hx, 0].astype(F32)
        s3[hx] = both.astype(BF16)
        send((stage, hx, 1), s3.at[hx], got.at[hx, 1], near(axis, lean))

    def reduce_end(stage, hx):
        got = into[stage]
        total = block(stage, hx, 0)[...].astype(F32)
        for n in range(1 if relayed(stage, hx) else 0, 3):
            arrived((stage, hx, n), got.at[hx, n])
            total = total + got[hx, n].astype(F32)
        if stage == 1:
            res1[hx] = total.astype(BF16)
        else:
            res2[:, hx] = total.astype(BF16).reshape(4, 16, total.shape[-1])

    build(0)
    reduce_first(1, 0)
    build(2)
    reduce_first(1, 2)
    key_second()
    for hx in range(4):
        share(early(hx), hx)
    build(1)
    for hx in range(4):
        share(1 - early(hx), hx, ("z1", 1 - early(hx), hx))
    build(3)
    for hx in range(4):
        share(2, hx, ("z2", hx))
    reduce_second(1, 0)
    reduce_second(1, 2)
    reduce_first(1, 1)
    reduce_first(1, 3)
    share_end(0)
    share_end(1)

    transposed = (((0,), (0,)), ((), ()))

    def shard_term(hx, step, shard):
        return lax.dot_general(table[hx, at("key", step)], shard, transposed, preferred_element_type=F32)

    for hx in range(4):
        qsum[hx] = shard_term(hx, 0, ks_ref[hx]) + shard_term(hx, -1, kbuf[0, hx]) + shard_term(hx, 1, kbuf[1, hx])
    share_end(2)
    for hx in range(4):
        total = qsum[hx] + shard_term(hx, 2, kbuf[2, hx])
        qg[:, hx * 256 : (hx + 1) * 256] = total.astype(BF16)

    def project(j):
        loads[j].wait()
        out = lax.dot_general(qg[...], wv[j * wide : (j + 1) * wide], (((1,), (1,)), ((), ())), preferred_element_type=F32)
        po[j] = out.astype(BF16).reshape(2, 2, 64, wide)
        send(("c1", j), po.at[j, :, 1 - c], c1.at[j], other_core)

    def pass_on(j):
        arrived(("c1", j), c1.at[j])
        c2s[j] = (po[j, 1 - zl, c].astype(F32) + c1[j, 1 - zl].astype(F32)).astype(BF16)
        send(("c2", j), c2s.at[j], c2r.at[j], other_chip)

    def finish(j):
        arrived(("c2", j), c2r.at[j])
        total = po[j, zl, c].astype(F32) + c1[j, zl].astype(F32) + c2r[j].astype(F32)
        in_out[:, j * wide : (j + 1) * wide] = total.astype(BF16)

    held = 2
    for j in range(CHUNKS):
        project(j)
        if j >= 2:
            pass_on(j - 2)
        if j in (2, 3):
            reduce_end(1, 2 * j - 4)
            reduce_first(2, 2 * j - 4)
    for hx in (1, 3):
        reduce_end(1, hx)
        reduce_first(2, hx)
    for j in range(2):
        finish(j)
    for hx in (0, 2, 1, 3):
        reduce_end(2, hx)
    for n, step in enumerate(OTHERS):
        send((3, n), res2.at[at("key", step)], r3.at[n], near("key", step))
    for j in range(CHUNKS - held, CHUNKS):
        pass_on(j)
    for j in range(2, CHUNKS):
        finish(j)
    total = res2[k].astype(F32)
    for n in range(3):
        arrived((3, n), r3.at[n])
        total = total + r3[n].astype(F32)
    key_out[...] = total
    for one in sent:
        one.wait_send()


def on_device(queries, sub_keys, query_weight, sub_choice, pair_choice, weights, weight_grad):
    tok, heads, halves, width = queries.shape
    topk = pair_choice.shape[2]
    groups = heads * halves
    rows = sub_keys.shape[0]
    model = query_weight.shape[0]
    wide = model // CHUNKS
    idx = jnp.transpose(sub_choice, (1, 2, 3, 0)).reshape(groups, topk, tok)
    pair, w, wg = (jnp.transpose(v, (1, 2, 0)) for v in (pair_choice, weights, weight_grad))
    vmem = pl.BlockSpec(memory_space=pltpu.VMEM)
    key_grad, in_grad = pl.pallas_call(
        kernel,
        out_shape=(
            jax.ShapeDtypeStruct((groups, 16, width), F32),
            jax.ShapeDtypeStruct((tok // 4, model), BF16),
        ),
        in_specs=[pl.BlockSpec(memory_space=pltpu.HBM)] * 7,
        out_specs=(vmem, vmem),
        scratch_shapes=[
            pltpu.VMEM(idx.shape, idx.dtype),
            pltpu.VMEM(pair.shape, pair.dtype),
            pltpu.VMEM(w.shape, w.dtype),
            pltpu.VMEM(wg.shape, wg.dtype),
            pltpu.VMEM(queries.shape, queries.dtype),
            pltpu.VMEM(sub_keys.shape, sub_keys.dtype),
            pltpu.VMEM((width // 128, 2 * tok, 128), F32),
            pltpu.VMEM((groups, tok, width), queries.dtype),
            pltpu.VMEM((groups, rows, width), sub_keys.dtype),
            pltpu.VMEM((groups, topk, tok), F32),
            pltpu.VMEM((groups, topk, tok), F32),
            pltpu.VMEM((topk, tok), F32),
            pltpu.VMEM((topk, tok), jnp.int32),
            pltpu.VMEM((topk, tok), jnp.int32),
            pltpu.VMEM((groups, 4, rows, tok), BF16),
            pltpu.VMEM((groups, 4, 4, 64, width), BF16),
            pltpu.VMEM((3, groups, rows, width), BF16),
            pltpu.VMEM((model, groups * width), BF16),
            pltpu.VMEM((tok, groups * width), BF16),
            pltpu.VMEM((groups, tok, width), F32),
            pltpu.VMEM((groups, 3, 4, 64, width), BF16),
            pltpu.VMEM((groups, 4, 64, width), BF16),
            pltpu.VMEM((groups, 4, 64, width), BF16),
            pltpu.VMEM((groups, 3, 64, width), BF16),
            pltpu.VMEM((4, groups, 16, width), BF16),
            pltpu.VMEM((3, groups, 16, width), BF16),
            pltpu.VMEM((CHUNKS, 2, 2, 64, wide), BF16),
            pltpu.VMEM((CHUNKS, 2, 64, wide), BF16),
            pltpu.VMEM((CHUNKS, 64, wide), BF16),
            pltpu.VMEM((CHUNKS, 64, wide), BF16),
            pltpu.SemaphoreType.DMA((CHUNKS,)),
            pltpu.SemaphoreType.DMA((6,)),
            pltpu.SemaphoreType.DMA((MESSAGES,)),
            pltpu.SemaphoreType.DMA((MESSAGES,)),
        ],
        compiler_params=pltpu.CompilerParams(
            collective_id=0, has_side_effects=True, vmem_limit_bytes=40000000
        ),
    )(*(pltpu.with_memory_space_constraint(v, pltpu.HBM) for v in (idx, pair, w, wg, queries, sub_keys, query_weight)))
    sub_key_grad = jnp.transpose(key_grad, (1, 0, 2)).reshape(16, heads, halves, width)
    return sub_key_grad, in_grad


def solution(mesh):
    split = Mesh(
        mesh.devices.reshape(4, 4, mesh.shape["key"], mesh.shape["tensor"]), AXES
    )
    in_specs = (
        P(DP_KEY, "tensor", None, None),
        P("key", "tensor", None, None),
        P(None, "tensor"),
        P(DP_KEY, "tensor", None, None),
        P(DP_KEY, "tensor", None),
        P(DP_KEY, "tensor", None),
        P(DP_KEY, "tensor", None),
    )
    out_specs = (P(DP_KEY, "tensor", None, None), P(DP_KEY_TENSOR, None))
    return jax.shard_map(
        on_device, mesh=split, in_specs=in_specs, out_specs=out_specs, check_vma=False
    )
```

```python
import functools

import jax
import jax.numpy as jnp
from jax import lax
from jax.experimental import pallas as pl
from jax.experimental.pallas import tpu as pltpu
from jax.sharding import Mesh
from jax.sharding import PartitionSpec as P

DP_KEY = ("dp_0", "dp_1", "key")
DP_KEY_TENSOR = ("dp_0", "dp_1", "key", "tensor")
AXES = ("dp_0", "dp_1", "key", "tensor")
MESH = pl.DeviceIdType.MESH
F32 = jnp.float32
BF16 = jnp.bfloat16
CHUNKS = 8
OTHERS = (2, 1, -1)
MESSAGES = 96


def kernel(
    idx_hbm, pair_hbm, w_hbm, wg_hbm, q_hbm, ks_hbm, wq_ref,
    key_out, in_out,
    idx_ref, pair_ref, w_ref, wg_ref, q_raw, ks_raw, pairs, q_ref, ks_ref,
    idxf, val, score, first, second, table, part, kbuf, wv, qg, qsum,
    r1, s3, res1, r2, res2, r3, po, c1, c2s, c2r,
    w_sem, in_sem, send_sem, recv_sem,
):
    y, x, k, t = (lax.axis_index(a) for a in AXES)
    zl, c = t // 2, lax.rem(t, 2)
    coord = {"dp_0": y, "dp_1": x, "key": k}

    def at(axis, step):
        return lax.rem(coord[axis] + step + 4, 4)

    def near(axis, step):
        return {axis: at(axis, step)}

    other_core = {"tensor": zl * 2 + (1 - c)}
    other_chip = {"tensor": (1 - zl) * 2 + c}

    barrier = pltpu.get_barrier_semaphore()
    partners = [near(a, s) for a in ("dp_0", "dp_1") for s in OTHERS]
    partners += [near("key", s) for s in OTHERS] + [other_core, other_chip]
    for device in partners:
        pl.semaphore_signal(barrier, inc=1, device_id=device, device_id_type=MESH)

    fetched = [
        pltpu.make_async_copy(src, dst, in_sem.at[n])
        for n, (src, dst) in enumerate((
            (ks_hbm, ks_raw), (w_hbm, w_ref), (wg_hbm, wg_ref),
            (pair_hbm, pair_ref), (idx_hbm, idx_ref), (q_hbm, q_raw),
        ))
    ]
    for one in fetched:
        one.start()
    wide = wv.shape[0] // CHUNKS
    loads = [
        pltpu.make_async_copy(wq_ref.at[pl.ds(j * wide, wide)], wv.at[pl.ds(j * wide, wide)], w_sem.at[j])
        for j in range(CHUNKS)
    ]
    for load in loads:
        load.start()
    fetched[0].wait()

    def lay_out(raw, dst):
        for h in range(2):
            both = raw[:, h].astype(F32).reshape(2 * raw.shape[0], raw.shape[3])
            for n in range(raw.shape[3] // 128):
                lanes = slice(n * 128, (n + 1) * 128)
                pairs[n] = both[:, lanes]
                for half in range(2):
                    dst[2 * h + half, :, lanes] = pairs[n, pl.ds(half, raw.shape[0], stride=2), :].astype(BF16)

    lay_out(ks_raw, ks_ref)
    pl.semaphore_wait(barrier, len(partners))

    names, sent = {}, []

    def copy(name, src, dst, device):
        n = names.setdefault(name, len(names))
        return pltpu.make_async_remote_copy(
            src_ref=src, dst_ref=dst, send_sem=send_sem.at[n], recv_sem=recv_sem.at[n],
            device_id=device, device_id_type=MESH,
        )

    def send(name, src, dst, device):
        one = copy(name, src, dst, device)
        one.start()
        sent.append(one)

    def arrived(name, dst):
        copy(name, dst, dst, other_core).wait_recv()

    def way(hx):
        return 1 - 2 * (hx % 2)

    rows = kbuf.shape[2] // 4

    def ring(hx):
        return "dp_1" if hx < 2 else "dp_0"

    def quarter(hx, step=0):
        return pl.ds(pl.multiple_of(at(ring(hx), step) * rows, rows), rows)

    def key_first(late):
        for hx in range(4):
            d = -way(hx) if late else way(hx)
            slot = (1 - d) // 2
            send(("z1", slot, hx), ks_ref.at[hx, quarter(hx)], kbuf.at[slot, hx, quarter(hx)], near("key", d))

    def key_second():
        for hx in range(4):
            d = way(hx)
            slot = (1 - d) // 2
            piece = kbuf.at[slot, hx, quarter(hx)]
            arrived(("z1", slot, hx), piece)
            send(("z2", hx), piece, kbuf.at[2, hx, quarter(hx)], near("key", d))

    def share(slot, hx, name=None):
        piece = kbuf.at[slot, hx, quarter(hx)]
        if name is not None:
            arrived(name, piece)
        for step in OTHERS if slot == 2 else (1, -1):
            send(("g", slot, hx, step), piece, piece, near(ring(hx), step))

    def share_second(slot, hx):
        d = way(hx)
        piece = kbuf.at[slot, hx, quarter(hx, -d)]
        arrived(("g", slot, hx, d), piece)
        send(("g", slot, hx, 2), piece, piece, near(ring(hx), d))

    def share_end(slot):
        for hx in range(4):
            for step in OTHERS:
                if slot == 2 or step != way(hx):
                    arrived(("g", slot, hx, step), kbuf.at[slot, hx, quarter(hx, -step)])

    def early(hx):
        return (1 - way(hx)) // 2

    key_first(False)
    key_first(True)

    for one in fetched[1:]:
        one.wait()
    lay_out(q_raw, q_ref)

    kept, tokens = idx_ref.shape[1], idx_ref.shape[2]
    for hx in range(4):
        idxf[hx] = idx_ref[hx].astype(F32)
    slots = lax.broadcasted_iota(jnp.int32, (kept, tokens), 0)
    for h in range(2):
        product = w_ref[h] * wg_ref[h]
        total = jnp.sum(product, axis=0, keepdims=True)
        score[...] = w_ref[h] * (wg_ref[h] - total)
        first[...] = pair_ref[h] >> 5
        second[...] = pair_ref[h] & 31

        def add_pairs(step, sums):
            one, two = sums
            for sub in range(4):
                row = pl.ds(step * 4 + sub, 1)
                here = score[row, :]
                one = one + jnp.where(slots == first[row, :], here, 0.0)
                two = two + jnp.where(slots == second[row, :], here, 0.0)
            return one, two

        zero = jnp.zeros((kept, tokens), F32)
        one, two = lax.fori_loop(0, kept // 4, add_pairs, (zero, zero))
        val[2 * h] = one
        val[2 * h + 1] = two

    across = 128
    ids = lax.broadcasted_iota(jnp.int32, (16, 16, across), 0) * 16 + lax.broadcasted_iota(jnp.int32, (16, 16, across), 1)
    ids = ids.astype(F32).astype(BF16)

    def build(hx):
        @pl.loop(0, 4)
        def _(b):
            low = (b * 256).astype(F32)
            for lane in range(tokens // across):
                cols = slice(lane * across, (lane + 1) * across)
                acc = jnp.zeros((16, 16, across), BF16)
                for a in range(kept):
                    place = jnp.broadcast_to(idxf[hx, a : a + 1, cols] - low, (16, across)).astype(BF16)
                    value = jnp.broadcast_to(val[hx, a : a + 1, cols], (16, across)).astype(BF16)
                    acc = jnp.where(ids == place[None], value[None], acc)
                table[hx, b, :, cols] = acc.reshape(256, across)
            grad = jnp.dot(table[hx, b], q_ref[hx], preferred_element_type=F32)
            part[hx, b] = grad.astype(BF16).reshape(4, 64, grad.shape[1])

    def block(stage, hx, step):
        if stage == 2:
            return res1.at[hx, at("dp_0" if hx < 2 else "dp_1", step)]
        if hx < 2:
            return part.at[hx, :, at("dp_1", step)]
        return part.at[hx, at("dp_0", step)]

    def axis_of(stage, hx):
        return "dp_1" if (hx < 2) == (stage == 1) else "dp_0"

    into = {1: r1, 2: r2}
    lean = 1 - 2 * c

    def relayed(stage, hx):
        return stage == 1 and hx % 2 == 0

    def reduce_first(stage, hx):
        axis, got = axis_of(stage, hx), into[stage]
        if relayed(stage, hx):
            send((stage, hx, 0), block(stage, hx, 2), got.at[hx, 0], near(axis, lean))
            send((stage, hx, 2), block(stage, hx, -lean), got.at[hx, 2], near(axis, -lean))
        else:
            for n, step in enumerate(OTHERS):
                send((stage, hx, n), block(stage, hx, step), got.at[hx, n], near(axis, step))

    def reduce_second(stage, hx):
        axis, got = axis_of(stage, hx), into[stage]
        arrived((stage, hx, 0), got.at[hx, 0])
        both = block(stage, hx, lean)[...].astype(F32) + got[hx, 0].astype(F32)
        s3[hx] = both.astype(BF16)
        send((stage, hx, 1), s3.at[hx], got.at[hx, 1], near(axis, lean))

    def reduce_end(stage, hx):
        got = into[stage]
        total = block(stage, hx, 0)[...].astype(F32)
        for n in range(1 if relayed(stage, hx) else 0, 3):
            arrived((stage, hx, n), got.at[hx, n])
            total = total + got[hx, n].astype(F32)
        if stage == 1:
            res1[hx] = total.astype(BF16)
        else:
            res2[:, hx % 2 * 2 + hx // 2] = total.astype(BF16).reshape(4, 16, total.shape[-1])

    build(0)
    reduce_first(1, 0)
    build(2)
    reduce_first(1, 2)
    key_second()
    for hx in range(4):
        share(early(hx), hx)
    build(1)
    for hx in range(4):
        share(1 - early(hx), hx, ("z1", 1 - early(hx), hx))
    build(3)
    for hx in range(4):
        share(2, hx, ("z2", hx))
    for hx in range(4):
        share_second(early(hx), hx)
    reduce_second(1, 0)
    reduce_second(1, 2)
    for hx in range(4):
        share_second(1 - early(hx), hx)
    reduce_first(1, 1)
    reduce_first(1, 3)
    share_end(0)
    share_end(1)

    transposed = (((0,), (0,)), ((), ()))

    def shard_term(hx, step, shard):
        return lax.dot_general(table[hx, at("key", step)], shard, transposed, preferred_element_type=F32)

    for hx in range(4):
        qsum[hx] = shard_term(hx, 0, ks_ref[hx]) + shard_term(hx, -1, kbuf[0, hx]) + shard_term(hx, 1, kbuf[1, hx])
    share_end(2)
    for hx in range(4):
        total = qsum[hx] + shard_term(hx, 2, kbuf[2, hx])
        qg[:, hx * 256 : (hx + 1) * 256] = total.astype(BF16)

    def project(j):
        loads[j].wait()
        out = lax.dot_general(qg[...], wv[j * wide : (j + 1) * wide], (((1,), (1,)), ((), ())), preferred_element_type=F32)
        po[j] = out.astype(BF16).reshape(2, 2, 64, wide)
        send(("c1", j), po.at[j, :, 1 - c], c1.at[j], other_core)

    def pass_on(j):
        arrived(("c1", j), c1.at[j])
        c2s[j] = (po[j, 1 - zl, c].astype(F32) + c1[j, 1 - zl].astype(F32)).astype(BF16)
        send(("c2", j), c2s.at[j], c2r.at[j], other_chip)

    def finish(j):
        arrived(("c2", j), c2r.at[j])
        total = po[j, zl, c].astype(F32) + c1[j, zl].astype(F32) + c2r[j].astype(F32)
        in_out[:, j * wide : (j + 1) * wide] = total.astype(BF16)

    def key_send(part):
        here = pl.ds(2 * part, 2)
        for n, step in enumerate(OTHERS):
            send((3, part, n), res2.at[at("key", step), here], r3.at[n, here], near("key", step))

    for j in range(CHUNKS):
        project(j)
        if j >= 2:
            pass_on(j - 2)
        if j in (2, 3):
            reduce_end(1, 2 * j - 4)
            reduce_first(2, 2 * j - 4)
    for hx in (1, 3):
        reduce_end(1, hx)
        reduce_first(2, hx)
        pass_on(CHUNKS - 2 + hx // 2)
    for part in range(2):
        for hx in (part, part + 2):
            reduce_end(2, hx)
        key_send(part)
    for j in range(CHUNKS):
        finish(j)
    for part in range(2):
        here = pl.ds(2 * part, 2)
        total = res2[k, here].astype(F32)
        for n in range(3):
            arrived((3, part, n), r3.at[n, here])
            total = total + r3[n, here].astype(F32)
        for n in range(2):
            key_out[part + 2 * n] = total[n]
    for one in sent:
        one.wait_send()


def on_device(queries, sub_keys, query_weight, sub_choice, pair_choice, weights, weight_grad):
    tok, heads, halves, width = queries.shape
    topk = pair_choice.shape[2]
    groups = heads * halves
    rows = sub_keys.shape[0]
    model = query_weight.shape[0]
    wide = model // CHUNKS
    idx = jnp.transpose(sub_choice, (1, 2, 3, 0)).reshape(groups, topk, tok)
    pair, w, wg = (jnp.transpose(v, (1, 2, 0)) for v in (pair_choice, weights, weight_grad))
    vmem = pl.BlockSpec(memory_space=pltpu.VMEM)
    key_grad, in_grad = pl.pallas_call(
        kernel,
        out_shape=(
            jax.ShapeDtypeStruct((groups, 16, width), F32),
            jax.ShapeDtypeStruct((tok // 4, model), BF16),
        ),
        in_specs=[pl.BlockSpec(memory_space=pltpu.HBM)] * 7,
        out_specs=(vmem, vmem),
        scratch_shapes=[
            pltpu.VMEM(idx.shape, idx.dtype),
            pltpu.VMEM(pair.shape, pair.dtype),
            pltpu.VMEM(w.shape, w.dtype),
            pltpu.VMEM(wg.shape, wg.dtype),
            pltpu.VMEM(queries.shape, queries.dtype),
            pltpu.VMEM(sub_keys.shape, sub_keys.dtype),
            pltpu.VMEM((width // 128, 2 * tok, 128), F32),
            pltpu.VMEM((groups, tok, width), queries.dtype),
            pltpu.VMEM((groups, rows, width), sub_keys.dtype),
            pltpu.VMEM((groups, topk, tok), F32),
            pltpu.VMEM((groups, topk, tok), F32),
            pltpu.VMEM((topk, tok), F32),
            pltpu.VMEM((topk, tok), jnp.int32),
            pltpu.VMEM((topk, tok), jnp.int32),
            pltpu.VMEM((groups, 4, rows, tok), BF16),
            pltpu.VMEM((groups, 4, 4, 64, width), BF16),
            pltpu.VMEM((3, groups, rows, width), BF16),
            pltpu.VMEM((model, groups * width), BF16),
            pltpu.VMEM((tok, groups * width), BF16),
            pltpu.VMEM((groups, tok, width), F32),
            pltpu.VMEM((groups, 3, 4, 64, width), BF16),
            pltpu.VMEM((groups, 4, 64, width), BF16),
            pltpu.VMEM((groups, 4, 64, width), BF16),
            pltpu.VMEM((groups, 3, 64, width), BF16),
            pltpu.VMEM((4, groups, 16, width), BF16),
            pltpu.VMEM((3, groups, 16, width), BF16),
            pltpu.VMEM((CHUNKS, 2, 2, 64, wide), BF16),
            pltpu.VMEM((CHUNKS, 2, 64, wide), BF16),
            pltpu.VMEM((CHUNKS, 64, wide), BF16),
            pltpu.VMEM((CHUNKS, 64, wide), BF16),
            pltpu.SemaphoreType.DMA((CHUNKS,)),
            pltpu.SemaphoreType.DMA((6,)),
            pltpu.SemaphoreType.DMA((MESSAGES,)),
            pltpu.SemaphoreType.DMA((MESSAGES,)),
        ],
        compiler_params=pltpu.CompilerParams(
            collective_id=0, has_side_effects=True, vmem_limit_bytes=40000000
        ),
    )(*(pltpu.with_memory_space_constraint(v, pltpu.HBM) for v in (idx, pair, w, wg, queries, sub_keys, query_weight)))
    sub_key_grad = jnp.transpose(key_grad, (1, 0, 2)).reshape(16, heads, halves, width)
    return sub_key_grad, in_grad


def solution(mesh):
    split = Mesh(
        mesh.devices.reshape(4, 4, mesh.shape["key"], mesh.shape["tensor"]), AXES
    )
    in_specs = (
        P(DP_KEY, "tensor", None, None),
        P("key", "tensor", None, None),
        P(None, "tensor"),
        P(DP_KEY, "tensor", None, None),
        P(DP_KEY, "tensor", None),
        P(DP_KEY, "tensor", None),
        P(DP_KEY, "tensor", None),
    )
    out_specs = (P(DP_KEY, "tensor", None, None), P(DP_KEY_TENSOR, None))
    return jax.shard_map(
        on_device, mesh=split, in_specs=in_specs, out_specs=out_specs, check_vma=False
    )
```

```python
import functools

import jax
import jax.numpy as jnp
from jax import lax
from jax.experimental import pallas as pl
from jax.experimental.pallas import tpu as pltpu
from jax.sharding import Mesh
from jax.sharding import PartitionSpec as P

DP_KEY = ("dp_0", "dp_1", "key")
DP_KEY_TENSOR = ("dp_0", "dp_1", "key", "tensor")
AXES = ("dp_0", "dp_1", "key", "tensor")
MESH = pl.DeviceIdType.MESH
F32 = jnp.float32
BF16 = jnp.bfloat16
CHUNKS = 8
OTHERS = (2, 1, -1)
MESSAGES = 96


def kernel(
    idx_hbm, pair_hbm, w_hbm, wg_hbm, q_hbm, ks_hbm, wq_ref,
    key_out, in_out,
    idx_ref, pair_ref, w_ref, wg_ref, q_raw, ks_raw, pairs, q_ref, ks_ref,
    idxf, val, score, first, second, table, part, kbuf, wv, qg, qsum,
    r1, s3, res1, r2, res2, r3, po, c1, c2s, c2r,
    w_sem, in_sem, send_sem, recv_sem,
):
    y, x, k, t = (lax.axis_index(a) for a in AXES)
    zl, c = t // 2, lax.rem(t, 2)
    coord = {"dp_0": y, "dp_1": x, "key": k}

    def at(axis, step):
        return lax.rem(coord[axis] + step + 4, 4)

    def near(axis, step):
        return {axis: at(axis, step)}

    other_core = {"tensor": zl * 2 + (1 - c)}
    other_chip = {"tensor": (1 - zl) * 2 + c}

    barrier = pltpu.get_barrier_semaphore()
    partners = [near(a, s) for a in ("dp_0", "dp_1") for s in OTHERS]
    partners += [near("key", s) for s in OTHERS] + [other_core, other_chip]
    for device in partners:
        pl.semaphore_signal(barrier, inc=1, device_id=device, device_id_type=MESH)

    fetched = [
        pltpu.make_async_copy(src, dst, in_sem.at[n])
        for n, (src, dst) in enumerate((
            (ks_hbm, ks_raw), (w_hbm, w_ref), (wg_hbm, wg_ref),
            (pair_hbm, pair_ref), (idx_hbm, idx_ref), (q_hbm, q_raw),
        ))
    ]
    for one in fetched:
        one.start()
    wide = wv.shape[0] // CHUNKS
    loads = [
        pltpu.make_async_copy(wq_ref.at[pl.ds(j * wide, wide)], wv.at[pl.ds(j * wide, wide)], w_sem.at[j])
        for j in range(CHUNKS)
    ]
    for load in loads:
        load.start()
    fetched[0].wait()

    def lay_out(raw, dst):
        for h in range(2):
            both = raw[:, h].astype(F32).reshape(2 * raw.shape[0], raw.shape[3])
            for n in range(raw.shape[3] // 128):
                lanes = slice(n * 128, (n + 1) * 128)
                pairs[n] = both[:, lanes]
                for half in range(2):
                    dst[2 * h + half, :, lanes] = pairs[n, pl.ds(half, raw.shape[0], stride=2), :].astype(BF16)

    lay_out(ks_raw, ks_ref)
    pl.semaphore_wait(barrier, len(partners))

    names, sent = {}, []

    def copy(name, src, dst, device):
        n = names.setdefault(name, len(names))
        return pltpu.make_async_remote_copy(
            src_ref=src, dst_ref=dst, send_sem=send_sem.at[n], recv_sem=recv_sem.at[n],
            device_id=device, device_id_type=MESH,
        )

    def send(name, src, dst, device):
        one = copy(name, src, dst, device)
        one.start()
        sent.append(one)

    def arrived(name, dst):
        copy(name, dst, dst, other_core).wait_recv()

    def way(hx):
        return 1 - 2 * (hx % 2)

    rows = kbuf.shape[2] // 4

    def ring(hx):
        return "dp_1" if hx < 2 else "dp_0"

    def quarter(hx, step=0):
        return pl.ds(pl.multiple_of(at(ring(hx), step) * rows, rows), rows)

    def key_first(late):
        for hx in range(4):
            d = -way(hx) if late else way(hx)
            slot = (1 - d) // 2
            send(("z1", slot, hx), ks_ref.at[hx, quarter(hx)], kbuf.at[slot, hx, quarter(hx)], near("key", d))

    def key_second():
        for hx in range(4):
            d = way(hx)
            slot = (1 - d) // 2
            piece = kbuf.at[slot, hx, quarter(hx)]
            arrived(("z1", slot, hx), piece)
            send(("z2", hx), piece, kbuf.at[2, hx, quarter(hx)], near("key", d))

    def share(slot, hx, name=None):
        piece = kbuf.at[slot, hx, quarter(hx)]
        if name is not None:
            arrived(name, piece)
        for step in OTHERS:
            send(("g", slot, hx, step), piece, piece, near(ring(hx), step))

    def share_end(slot):
        for hx in range(4):
            for step in OTHERS:
                arrived(("g", slot, hx, step), kbuf.at[slot, hx, quarter(hx, -step)])

    def early(hx):
        return (1 - way(hx)) // 2

    key_first(False)
    key_first(True)

    for one in fetched[1:]:
        one.wait()
    lay_out(q_raw, q_ref)

    kept, tokens = idx_ref.shape[1], idx_ref.shape[2]
    for hx in range(4):
        idxf[hx] = idx_ref[hx].astype(F32)
    slots = lax.broadcasted_iota(jnp.int32, (kept, tokens), 0)
    for h in range(2):
        product = w_ref[h] * wg_ref[h]
        total = jnp.sum(product, axis=0, keepdims=True)
        score[...] = w_ref[h] * (wg_ref[h] - total)
        first[...] = pair_ref[h] >> 5
        second[...] = pair_ref[h] & 31

        def add_pairs(step, sums):
            one, two = sums
            for sub in range(4):
                row = pl.ds(step * 4 + sub, 1)
                here = score[row, :]
                one = one + jnp.where(slots == first[row, :], here, 0.0)
                two = two + jnp.where(slots == second[row, :], here, 0.0)
            return one, two

        zero = jnp.zeros((kept, tokens), F32)
        one, two = lax.fori_loop(0, kept // 4, add_pairs, (zero, zero))
        val[2 * h] = one
        val[2 * h + 1] = two

    across = 128
    ids = lax.broadcasted_iota(jnp.int32, (16, 16, across), 0) * 16 + lax.broadcasted_iota(jnp.int32, (16, 16, across), 1)
    ids = ids.astype(F32).astype(BF16)

    def build(hx):
        @pl.loop(0, 4)
        def _(b):
            low = (b * 256).astype(F32)
            for lane in range(tokens // across):
                cols = slice(lane * across, (lane + 1) * across)
                acc = jnp.zeros((16, 16, across), BF16)
                for a in range(kept):
                    place = jnp.broadcast_to(idxf[hx, a : a + 1, cols] - low, (16, across)).astype(BF16)
                    value = jnp.broadcast_to(val[hx, a : a + 1, cols], (16, across)).astype(BF16)
                    acc = jnp.where(ids == place[None], value[None], acc)
                table[hx, b, :, cols] = acc.reshape(256, across)
            grad = jnp.dot(table[hx, b], q_ref[hx], preferred_element_type=F32)
            part[hx, b] = grad.astype(BF16).reshape(4, 64, grad.shape[1])

    def block(stage, hx, step):
        if stage == 2:
            return res1.at[hx, at("dp_0" if hx < 2 else "dp_1", step)]
        if hx < 2:
            return part.at[hx, :, at("dp_1", step)]
        return part.at[hx, at("dp_0", step)]

    def axis_of(stage, hx):
        return "dp_1" if (hx < 2) == (stage == 1) else "dp_0"

    into = {1: r1, 2: r2}
    lean = 1 - 2 * c

    def relayed(stage, hx):
        return stage == 1 and hx % 2 == 0

    def reduce_first(stage, hx):
        axis, got = axis_of(stage, hx), into[stage]
        if relayed(stage, hx):
            send((stage, hx, 0), block(stage, hx, 2), got.at[hx, 0], near(axis, lean))
            send((stage, hx, 2), block(stage, hx, -lean), got.at[hx, 2], near(axis, -lean))
        else:
            for n, step in enumerate(OTHERS):
                send((stage, hx, n), block(stage, hx, step), got.at[hx, n], near(axis, step))

    def reduce_second(stage, hx):
        axis, got = axis_of(stage, hx), into[stage]
        arrived((stage, hx, 0), got.at[hx, 0])
        both = block(stage, hx, lean)[...].astype(F32) + got[hx, 0].astype(F32)
        s3[hx] = both.astype(BF16)
        send((stage, hx, 1), s3.at[hx], got.at[hx, 1], near(axis, lean))

    def reduce_end(stage, hx):
        got = into[stage]
        total = block(stage, hx, 0)[...].astype(F32)
        for n in range(1 if relayed(stage, hx) else 0, 3):
            arrived((stage, hx, n), got.at[hx, n])
            total = total + got[hx, n].astype(F32)
        if stage == 1:
            res1[hx] = total.astype(BF16)
        else:
            res2[:, hx % 2 * 2 + hx // 2] = total.astype(BF16).reshape(4, 16, total.shape[-1])

    build(0)
    reduce_first(1, 0)
    build(2)
    reduce_first(1, 2)
    key_second()
    for hx in range(4):
        share(early(hx), hx)
    build(1)
    for hx in range(4):
        share(1 - early(hx), hx, ("z1", 1 - early(hx), hx))
    build(3)
    for hx in range(4):
        share(2, hx, ("z2", hx))
    reduce_second(1, 0)
    reduce_second(1, 2)
    reduce_first(1, 1)
    reduce_first(1, 3)
    share_end(0)
    share_end(1)

    transposed = (((0,), (0,)), ((), ()))

    def shard_term(hx, step, shard):
        return lax.dot_general(table[hx, at("key", step)], shard, transposed, preferred_element_type=F32)

    for hx in range(4):
        qsum[hx] = shard_term(hx, 0, ks_ref[hx]) + shard_term(hx, -1, kbuf[0, hx]) + shard_term(hx, 1, kbuf[1, hx])
    share_end(2)
    for hx in range(4):
        total = qsum[hx] + shard_term(hx, 2, kbuf[2, hx])
        qg[:, hx * 256 : (hx + 1) * 256] = total.astype(BF16)

    def project(j):
        loads[j].wait()
        out = lax.dot_general(qg[...], wv[j * wide : (j + 1) * wide], (((1,), (1,)), ((), ())), preferred_element_type=F32)
        po[j] = out.astype(BF16).reshape(2, 2, 64, wide)
        send(("c1", j), po.at[j, :, 1 - c], c1.at[j], other_core)

    def pass_on(j):
        arrived(("c1", j), c1.at[j])
        c2s[j] = (po[j, 1 - zl, c].astype(F32) + c1[j, 1 - zl].astype(F32)).astype(BF16)
        send(("c2", j), c2s.at[j], c2r.at[j], other_chip)

    def finish(j):
        arrived(("c2", j), c2r.at[j])
        total = po[j, zl, c].astype(F32) + c1[j, zl].astype(F32) + c2r[j].astype(F32)
        in_out[:, j * wide : (j + 1) * wide] = total.astype(BF16)

    def key_send(part):
        here = pl.ds(2 * part, 2)
        for n, step in enumerate(OTHERS):
            send((3, part, n), res2.at[at("key", step), here], r3.at[n, here], near("key", step))

    for j in range(CHUNKS):
        project(j)
        if j >= 2:
            pass_on(j - 2)
        if j in (2, 3):
            reduce_end(1, 2 * j - 4)
            reduce_first(2, 2 * j - 4)
    for hx in (1, 3):
        reduce_end(1, hx)
        reduce_first(2, hx)
        pass_on(CHUNKS - 2 + hx // 2)
    for part in range(2):
        for hx in (part, part + 2):
            reduce_end(2, hx)
        key_send(part)
    for j in range(CHUNKS):
        finish(j)
    for part in range(2):
        here = pl.ds(2 * part, 2)
        total = res2[k, here].astype(F32)
        for n in range(3):
            arrived((3, part, n), r3.at[n, here])
            total = total + r3[n, here].astype(F32)
        for n in range(2):
            key_out[part + 2 * n] = total[n]
    for one in sent:
        one.wait_send()


def on_device(queries, sub_keys, query_weight, sub_choice, pair_choice, weights, weight_grad):
    tok, heads, halves, width = queries.shape
    topk = pair_choice.shape[2]
    groups = heads * halves
    rows = sub_keys.shape[0]
    model = query_weight.shape[0]
    wide = model // CHUNKS
    idx = jnp.transpose(sub_choice, (1, 2, 3, 0)).reshape(groups, topk, tok)
    pair, w, wg = (jnp.transpose(v, (1, 2, 0)) for v in (pair_choice, weights, weight_grad))
    vmem = pl.BlockSpec(memory_space=pltpu.VMEM)
    key_grad, in_grad = pl.pallas_call(
        kernel,
        out_shape=(
            jax.ShapeDtypeStruct((groups, 16, width), F32),
            jax.ShapeDtypeStruct((tok // 4, model), BF16),
        ),
        in_specs=[pl.BlockSpec(memory_space=pltpu.HBM)] * 7,
        out_specs=(vmem, vmem),
        scratch_shapes=[
            pltpu.VMEM(idx.shape, idx.dtype),
            pltpu.VMEM(pair.shape, pair.dtype),
            pltpu.VMEM(w.shape, w.dtype),
            pltpu.VMEM(wg.shape, wg.dtype),
            pltpu.VMEM(queries.shape, queries.dtype),
            pltpu.VMEM(sub_keys.shape, sub_keys.dtype),
            pltpu.VMEM((width // 128, 2 * tok, 128), F32),
            pltpu.VMEM((groups, tok, width), queries.dtype),
            pltpu.VMEM((groups, rows, width), sub_keys.dtype),
            pltpu.VMEM((groups, topk, tok), F32),
            pltpu.VMEM((groups, topk, tok), F32),
            pltpu.VMEM((topk, tok), F32),
            pltpu.VMEM((topk, tok), jnp.int32),
            pltpu.VMEM((topk, tok), jnp.int32),
            pltpu.VMEM((groups, 4, rows, tok), BF16),
            pltpu.VMEM((groups, 4, 4, 64, width), BF16),
            pltpu.VMEM((3, groups, rows, width), BF16),
            pltpu.VMEM((model, groups * width), BF16),
            pltpu.VMEM((tok, groups * width), BF16),
            pltpu.VMEM((groups, tok, width), F32),
            pltpu.VMEM((groups, 3, 4, 64, width), BF16),
            pltpu.VMEM((groups, 4, 64, width), BF16),
            pltpu.VMEM((groups, 4, 64, width), BF16),
            pltpu.VMEM((groups, 3, 64, width), BF16),
            pltpu.VMEM((4, groups, 16, width), BF16),
            pltpu.VMEM((3, groups, 16, width), BF16),
            pltpu.VMEM((CHUNKS, 2, 2, 64, wide), BF16),
            pltpu.VMEM((CHUNKS, 2, 64, wide), BF16),
            pltpu.VMEM((CHUNKS, 64, wide), BF16),
            pltpu.VMEM((CHUNKS, 64, wide), BF16),
            pltpu.SemaphoreType.DMA((CHUNKS,)),
            pltpu.SemaphoreType.DMA((6,)),
            pltpu.SemaphoreType.DMA((MESSAGES,)),
            pltpu.SemaphoreType.DMA((MESSAGES,)),
        ],
        compiler_params=pltpu.CompilerParams(
            collective_id=0, has_side_effects=True, vmem_limit_bytes=40000000
        ),
    )(*(pltpu.with_memory_space_constraint(v, pltpu.HBM) for v in (idx, pair, w, wg, queries, sub_keys, query_weight)))
    sub_key_grad = jnp.transpose(key_grad, (1, 0, 2)).reshape(16, heads, halves, width)
    return sub_key_grad, in_grad


def solution(mesh):
    split = Mesh(
        mesh.devices.reshape(4, 4, mesh.shape["key"], mesh.shape["tensor"]), AXES
    )
    in_specs = (
        P(DP_KEY, "tensor", None, None),
        P("key", "tensor", None, None),
        P(None, "tensor"),
        P(DP_KEY, "tensor", None, None),
        P(DP_KEY, "tensor", None),
        P(DP_KEY, "tensor", None),
        P(DP_KEY, "tensor", None),
    )
    out_specs = (P(DP_KEY, "tensor", None, None), P(DP_KEY_TENSOR, None))
    return jax.shard_map(
        on_device, mesh=split, in_specs=in_specs, out_specs=out_specs, check_vma=False
    )
```

```python
import functools

import jax
import jax.numpy as jnp
from jax import lax
from jax.experimental import pallas as pl
from jax.experimental.pallas import tpu as pltpu
from jax.sharding import Mesh
from jax.sharding import PartitionSpec as P

DP_KEY = ("dp_0", "dp_1", "key")
DP_KEY_TENSOR = ("dp_0", "dp_1", "key", "tensor")
AXES = ("dp_0", "dp_1", "key", "tensor")
MESH = pl.DeviceIdType.MESH
F32 = jnp.float32
BF16 = jnp.bfloat16
CHUNKS = 8
OTHERS = (2, 1, -1)
MESSAGES = 96


def kernel(
    idx_hbm, pair_hbm, w_hbm, wg_hbm, q_hbm, ks_hbm, wq_ref,
    key_out, in_out,
    idx_ref, pair_ref, w_ref, wg_ref, q_raw, ks_raw, pairs, q_ref, ks_ref,
    idxf, val, score, first, second, table, part, kbuf, wv, qg, qsum,
    r1, s3, res1, r2, res2, r3, po, c1, c2s, c2r,
    w_sem, in_sem, send_sem, recv_sem,
):
    y, x, k, t = (lax.axis_index(a) for a in AXES)
    zl, c = t // 2, lax.rem(t, 2)
    coord = {"dp_0": y, "dp_1": x, "key": k}

    def at(axis, step):
        return lax.rem(coord[axis] + step + 4, 4)

    def near(axis, step):
        return {axis: at(axis, step)}

    other_core = {"tensor": zl * 2 + (1 - c)}
    other_chip = {"tensor": (1 - zl) * 2 + c}

    barrier = pltpu.get_barrier_semaphore()
    partners = [near(a, s) for a in ("dp_0", "dp_1") for s in OTHERS]
    partners += [near("key", s) for s in OTHERS] + [other_core, other_chip]
    for device in partners:
        pl.semaphore_signal(barrier, inc=1, device_id=device, device_id_type=MESH)

    fetched = [
        pltpu.make_async_copy(src, dst, in_sem.at[n])
        for n, (src, dst) in enumerate((
            (ks_hbm, ks_raw), (w_hbm, w_ref), (wg_hbm, wg_ref),
            (pair_hbm, pair_ref), (idx_hbm, idx_ref), (q_hbm, q_raw),
        ))
    ]
    for one in fetched:
        one.start()
    wide = wv.shape[0] // CHUNKS
    loads = [
        pltpu.make_async_copy(wq_ref.at[pl.ds(j * wide, wide)], wv.at[pl.ds(j * wide, wide)], w_sem.at[j])
        for j in range(CHUNKS)
    ]
    for load in loads:
        load.start()
    fetched[0].wait()

    def lay_out(raw, dst):
        for h in range(2):
            both = raw[:, h].astype(F32).reshape(2 * raw.shape[0], raw.shape[3])
            for n in range(raw.shape[3] // 128):
                lanes = slice(n * 128, (n + 1) * 128)
                pairs[n] = both[:, lanes]
                for half in range(2):
                    dst[2 * h + half, :, lanes] = pairs[n, pl.ds(half, raw.shape[0], stride=2), :].astype(BF16)

    lay_out(ks_raw, ks_ref)
    pl.semaphore_wait(barrier, len(partners))

    names, sent = {}, []

    def copy(name, src, dst, device):
        n = names.setdefault(name, len(names))
        return pltpu.make_async_remote_copy(
            src_ref=src, dst_ref=dst, send_sem=send_sem.at[n], recv_sem=recv_sem.at[n],
            device_id=device, device_id_type=MESH,
        )

    def send(name, src, dst, device):
        one = copy(name, src, dst, device)
        one.start()
        sent.append(one)

    def arrived(name, dst):
        copy(name, dst, dst, other_core).wait_recv()

    def way(hx):
        return 1 - 2 * (hx % 2)

    rows = kbuf.shape[2] // 4

    def ring(hx):
        return "dp_1" if hx < 2 else "dp_0"

    def quarter(hx, step=0):
        return pl.ds(pl.multiple_of(at(ring(hx), step) * rows, rows), rows)

    def key_first(late):
        for hx in range(4):
            d = -way(hx) if late else way(hx)
            slot = (1 - d) // 2
            send(("z1", slot, hx), ks_ref.at[hx, quarter(hx)], kbuf.at[slot, hx, quarter(hx)], near("key", d))

    def key_second():
        for hx in range(4):
            d = way(hx)
            slot = (1 - d) // 2
            piece = kbuf.at[slot, hx, quarter(hx)]
            arrived(("z1", slot, hx), piece)
            send(("z2", hx), piece, kbuf.at[2, hx, quarter(hx)], near("key", d))

    def share(slot, hx, name=None):
        piece = kbuf.at[slot, hx, quarter(hx)]
        if name is not None:
            arrived(name, piece)
        for step in OTHERS:
            send(("g", slot, hx, step), piece, piece, near(ring(hx), step))

    def share_end(slot):
        for hx in range(4):
            for step in OTHERS:
                arrived(("g", slot, hx, step), kbuf.at[slot, hx, quarter(hx, -step)])

    def early(hx):
        return (1 - way(hx)) // 2

    key_first(False)
    key_first(True)

    for one in fetched[1:]:
        one.wait()
    lay_out(q_raw, q_ref)

    kept, tokens = idx_ref.shape[1], idx_ref.shape[2]
    for hx in range(4):
        idxf[hx] = idx_ref[hx].astype(F32)
    slots = lax.broadcasted_iota(jnp.int32, (kept, tokens), 0)
    for h in range(2):
        product = w_ref[h] * wg_ref[h]
        total = jnp.sum(product, axis=0, keepdims=True)
        score[...] = w_ref[h] * (wg_ref[h] - total)
        first[...] = pair_ref[h] >> 5
        second[...] = pair_ref[h] & 31

        def add_pairs(step, sums):
            one, two = sums
            for sub in range(4):
                row = pl.ds(step * 4 + sub, 1)
                here = score[row, :]
                one = one + jnp.where(slots == first[row, :], here, 0.0)
                two = two + jnp.where(slots == second[row, :], here, 0.0)
            return one, two

        zero = jnp.zeros((kept, tokens), F32)
        one, two = lax.fori_loop(0, kept // 4, add_pairs, (zero, zero))
        val[2 * h] = one
        val[2 * h + 1] = two

    across = 128
    ids = lax.broadcasted_iota(jnp.int32, (16, 16, across), 0) * 16 + lax.broadcasted_iota(jnp.int32, (16, 16, across), 1)
    ids = ids.astype(F32).astype(BF16)

    def build(hx):
        @pl.loop(0, 4)
        def _(b):
            low = (b * 256).astype(F32)
            for lane in range(tokens // across):
                cols = slice(lane * across, (lane + 1) * across)
                acc = jnp.zeros((16, 16, across), BF16)
                for a in range(kept):
                    place = jnp.broadcast_to(idxf[hx, a : a + 1, cols] - low, (16, across)).astype(BF16)
                    value = jnp.broadcast_to(val[hx, a : a + 1, cols], (16, across)).astype(BF16)
                    acc = jnp.where(ids == place[None], value[None], acc)
                table[hx, b, :, cols] = acc.reshape(256, across)
            grad = jnp.dot(table[hx, b], q_ref[hx], preferred_element_type=F32)
            part[hx, b] = grad.astype(BF16).reshape(4, 64, grad.shape[1])

    def block(stage, hx, step):
        if stage == 2:
            return res1.at[hx, at("dp_0" if hx < 2 else "dp_1", step)]
        if hx < 2:
            return part.at[hx, :, at("dp_1", step)]
        return part.at[hx, at("dp_0", step)]

    def axis_of(stage, hx):
        return "dp_1" if (hx < 2) == (stage == 1) else "dp_0"

    into = {1: r1, 2: r2}
    lean = 1 - 2 * c

    def relayed(stage, hx):
        return stage == 1 and hx % 2 == 0

    def reduce_first(stage, hx):
        axis, got = axis_of(stage, hx), into[stage]
        if relayed(stage, hx):
            send((stage, hx, 0), block(stage, hx, 2), got.at[hx, 0], near(axis, lean))
            send((stage, hx, 2), block(stage, hx, -lean), got.at[hx, 2], near(axis, -lean))
        else:
            for n, step in enumerate(OTHERS):
                send((stage, hx, n), block(stage, hx, step), got.at[hx, n], near(axis, step))

    def reduce_second(stage, hx):
        axis, got = axis_of(stage, hx), into[stage]
        arrived((stage, hx, 0), got.at[hx, 0])
        both = block(stage, hx, lean)[...].astype(F32) + got[hx, 0].astype(F32)
        s3[hx] = both.astype(BF16)
        send((stage, hx, 1), s3.at[hx], got.at[hx, 1], near(axis, lean))

    def reduce_end(stage, hx):
        got = into[stage]
        total = block(stage, hx, 0)[...].astype(F32)
        for n in range(1 if relayed(stage, hx) else 0, 3):
            arrived((stage, hx, n), got.at[hx, n])
            total = total + got[hx, n].astype(F32)
        if stage == 1:
            res1[hx] = total.astype(BF16)
        else:
            res2[:, hx % 2 * 2 + hx // 2] = total.astype(BF16).reshape(4, 16, total.shape[-1])

    build(0)
    reduce_first(1, 0)
    build(2)
    reduce_first(1, 2)
    key_second()
    for hx in range(4):
        share(early(hx), hx)
    build(1)
    for hx in range(4):
        share(1 - early(hx), hx, ("z1", 1 - early(hx), hx))
    build(3)
    for hx in range(4):
        share(2, hx, ("z2", hx))
    reduce_second(1, 0)
    reduce_second(1, 2)
    reduce_first(1, 1)
    reduce_first(1, 3)
    share_end(0)
    share_end(1)

    transposed = (((0,), (0,)), ((), ()))

    def shard_term(hx, step, shard):
        return lax.dot_general(table[hx, at("key", step)], shard, transposed, preferred_element_type=F32)

    for hx in range(4):
        qsum[hx] = shard_term(hx, 0, ks_ref[hx]) + shard_term(hx, -1, kbuf[0, hx]) + shard_term(hx, 1, kbuf[1, hx])
    share_end(2)
    for hx in range(4):
        total = qsum[hx] + shard_term(hx, 2, kbuf[2, hx])
        qg[:, hx * 256 : (hx + 1) * 256] = total.astype(BF16)

    def project(j):
        loads[j].wait()
        out = lax.dot_general(qg[...], wv[j * wide : (j + 1) * wide], (((1,), (1,)), ((), ())), preferred_element_type=F32)
        po[j] = out.astype(BF16).reshape(2, 2, 64, wide)
        send(("c1", j), po.at[j, :, 1 - c], c1.at[j], other_core)

    def pass_on(j):
        arrived(("c1", j), c1.at[j])
        c2s[j] = (po[j, 1 - zl, c].astype(F32) + c1[j, 1 - zl].astype(F32)).astype(BF16)
        send(("c2", j), c2s.at[j], c2r.at[j], other_chip)

    def finish(j):
        arrived(("c2", j), c2r.at[j])
        total = po[j, zl, c].astype(F32) + c1[j, zl].astype(F32) + c2r[j].astype(F32)
        in_out[:, j * wide : (j + 1) * wide] = total.astype(BF16)

    def key_send(part):
        here = pl.ds(2 * part, 2)
        for n, step in enumerate(OTHERS):
            send((3, part, n), res2.at[at("key", step), here], r3.at[n, here], near("key", step))

    for j in range(CHUNKS):
        project(j)
        if 2 <= j < CHUNKS - 2:
            pass_on(j - 2)
        if j in (2, 3):
            reduce_end(1, 2 * j - 4)
            reduce_first(2, 2 * j - 4)
    for hx in (1, 3):
        reduce_end(1, hx)
        reduce_first(2, hx)
    for part in range(2):
        for hx in (part, part + 2):
            reduce_end(2, hx)
        key_send(part)
    for j in range(CHUNKS - 4, CHUNKS):
        pass_on(j)
    for j in range(CHUNKS):
        finish(j)
    for part in range(2):
        here = pl.ds(2 * part, 2)
        total = res2[k, here].astype(F32)
        for n in range(3):
            arrived((3, part, n), r3.at[n, here])
            total = total + r3[n, here].astype(F32)
        for n in range(2):
            key_out[part + 2 * n] = total[n]
    for one in sent:
        one.wait_send()


def on_device(queries, sub_keys, query_weight, sub_choice, pair_choice, weights, weight_grad):
    tok, heads, halves, width = queries.shape
    topk = pair_choice.shape[2]
    groups = heads * halves
    rows = sub_keys.shape[0]
    model = query_weight.shape[0]
    wide = model // CHUNKS
    idx = jnp.transpose(sub_choice, (1, 2, 3, 0)).reshape(groups, topk, tok)
    pair, w, wg = (jnp.transpose(v, (1, 2, 0)) for v in (pair_choice, weights, weight_grad))
    vmem = pl.BlockSpec(memory_space=pltpu.VMEM)
    key_grad, in_grad = pl.pallas_call(
        kernel,
        out_shape=(
            jax.ShapeDtypeStruct((groups, 16, width), F32),
            jax.ShapeDtypeStruct((tok // 4, model), BF16),
        ),
        in_specs=[pl.BlockSpec(memory_space=pltpu.HBM)] * 7,
        out_specs=(vmem, vmem),
        scratch_shapes=[
            pltpu.VMEM(idx.shape, idx.dtype),
            pltpu.VMEM(pair.shape, pair.dtype),
            pltpu.VMEM(w.shape, w.dtype),
            pltpu.VMEM(wg.shape, wg.dtype),
            pltpu.VMEM(queries.shape, queries.dtype),
            pltpu.VMEM(sub_keys.shape, sub_keys.dtype),
            pltpu.VMEM((width // 128, 2 * tok, 128), F32),
            pltpu.VMEM((groups, tok, width), queries.dtype),
            pltpu.VMEM((groups, rows, width), sub_keys.dtype),
            pltpu.VMEM((groups, topk, tok), F32),
            pltpu.VMEM((groups, topk, tok), F32),
            pltpu.VMEM((topk, tok), F32),
            pltpu.VMEM((topk, tok), jnp.int32),
            pltpu.VMEM((topk, tok), jnp.int32),
            pltpu.VMEM((groups, 4, rows, tok), BF16),
            pltpu.VMEM((groups, 4, 4, 64, width), BF16),
            pltpu.VMEM((3, groups, rows, width), BF16),
            pltpu.VMEM((model, groups * width), BF16),
            pltpu.VMEM((tok, groups * width), BF16),
            pltpu.VMEM((groups, tok, width), F32),
            pltpu.VMEM((groups, 3, 4, 64, width), BF16),
            pltpu.VMEM((groups, 4, 64, width), BF16),
            pltpu.VMEM((groups, 4, 64, width), BF16),
            pltpu.VMEM((groups, 3, 64, width), BF16),
            pltpu.VMEM((4, groups, 16, width), BF16),
            pltpu.VMEM((3, groups, 16, width), BF16),
            pltpu.VMEM((CHUNKS, 2, 2, 64, wide), BF16),
            pltpu.VMEM((CHUNKS, 2, 64, wide), BF16),
            pltpu.VMEM((CHUNKS, 64, wide), BF16),
            pltpu.VMEM((CHUNKS, 64, wide), BF16),
            pltpu.SemaphoreType.DMA((CHUNKS,)),
            pltpu.SemaphoreType.DMA((6,)),
            pltpu.SemaphoreType.DMA((MESSAGES,)),
            pltpu.SemaphoreType.DMA((MESSAGES,)),
        ],
        compiler_params=pltpu.CompilerParams(
            collective_id=0, has_side_effects=True, vmem_limit_bytes=40000000
        ),
    )(*(pltpu.with_memory_space_constraint(v, pltpu.HBM) for v in (idx, pair, w, wg, queries, sub_keys, query_weight)))
    sub_key_grad = jnp.transpose(key_grad, (1, 0, 2)).reshape(16, heads, halves, width)
    return sub_key_grad, in_grad


def solution(mesh):
    split = Mesh(
        mesh.devices.reshape(4, 4, mesh.shape["key"], mesh.shape["tensor"]), AXES
    )
    in_specs = (
        P(DP_KEY, "tensor", None, None),
        P("key", "tensor", None, None),
        P(None, "tensor"),
        P(DP_KEY, "tensor", None, None),
        P(DP_KEY, "tensor", None),
        P(DP_KEY, "tensor", None),
        P(DP_KEY, "tensor", None),
    )
    out_specs = (P(DP_KEY, "tensor", None, None), P(DP_KEY_TENSOR, None))
    return jax.shard_map(
        on_device, mesh=split, in_specs=in_specs, out_specs=out_specs, check_vma=False
    )
```
